32 devices in a mesh: nest: 2 (over core), rows: 8 (over z, x), sub: 2 (over y).
Axes of the slice: x: 2, y: 2, z: 4, core: 2. Of those that a mesh axis runs over, the one named last changes fastest.
Arguments:
- elevation: float32 [2, 1024, 1024], P('nest', ('rows', 'sub')), may hold values from -6 to 6
- momentum_x: float32 [2, 1024, 1024], P('nest', ('rows', 'sub')), may hold values from -6 to 6
- momentum_y: float32 [2, 1024, 1024], P('nest', ('rows', 'sub')), may hold values from -6 to 6
- depth: float32 [2, 1024, 1024], P('nest', ('rows', 'sub')), may hold values from 0.2 to 1
- wet_mask: int32 [2, 1024, 1024], P('nest', ('rows', 'sub')), may hold values 0 or 1
- inverse_x: float32 [2, 8, 128, 128], P('nest'), may hold values from -1 to 2, as said below
- inverse_y: float32 [2, 8, 128, 128], P('nest'), may hold values from -1 to 2, as said below
- nest_map: int32 [2, 2, 1024], replicated, may hold values from 0 to 1023, as said below
Outputs:
- elevation_out: float32 [2, 1024, 1024], P('nest', ('rows', 'sub'))
- momentum_x_out: float32 [2, 1024, 1024], P('nest', ('rows', 'sub'))
- momentum_y_out: float32 [2, 1024, 1024], P('nest', ('rows', 'sub'))
The draws below stay inside these ranges and needn't reach their ends.
Inputs may be any that keep to these rules, and one draw needn't show every extreme that they name: nest_map[b, 0, j] is the regional row and nest_map[b, 1, j] the regional column for cell j of the near-field's first (b = 0) or last (b = 1) row; the first row is driven by regional row 0 and the last by regional row 1023, and the column is c0 + j // 2 for one offset c0 shared by both rows, with every column below 1024. `inverse_x`: dense blocks, one for each line block of a section. `inverse_y`: dense blocks, one for each line block of a section.
All inputs are finite; a program needn't handle non-finite values. No bound on the sum of `wet_mask` on one device may be relied on, other than what follows from the above.
Results may differ from the reference program's by a relative error of at most 0.00013.
Values sent between devices are 32-bit elements; how exact they have to be, the bound alone decides.
No kernel may reach another device: no remote copies, remote signals or barrier semaphores. Data moves between devices by JAX's collectives and lax.ppermute only.
A program may use at most 64 MiB of HBM per device.

```python
import math
import jax
import jax.numpy as jnp
from jax import lax

GROUP = 128
STEPS = 2
NX = 1024
NY = 1024


def block_tables(key, count, noise):
    diagonal = jax.random.uniform(jax.random.fold_in(key, 11), (2, count, GROUP), jnp.float32, 0.5, 1.0)
    identity = jnp.eye(GROUP, dtype=jnp.float32)
    return diagonal[..., None] * identity + 0.25 / math.sqrt(GROUP) * noise


def draw_inverse_x(key, part):
    shape = (2, NX // GROUP, GROUP, GROUP)
    noise_key = jax.random.fold_in(key, 12)
    noise = jnp.clip(jax.random.normal(noise_key, shape, jnp.float32), -3.0, 3.0)
    return block_tables(key, NX // GROUP, noise).astype(jnp.float32)


def draw_inverse_y(key, part):
    shape = (2, NY // GROUP, GROUP, GROUP)
    noise_key = jax.random.fold_in(key, 13)
    noise = jnp.clip(jax.random.normal(noise_key, shape, jnp.float32), -3.0, 3.0)
    return block_tables(jax.random.fold_in(key, 14), NY // GROUP, noise).astype(jnp.float32)


def draw_nest_map(key, part):
    offset_top = min(NX // 2, NY - NX // 2)
    column_base = jax.random.randint(jax.random.fold_in(key, 23), (), 0, offset_top + 1)
    columns = column_base + jnp.arange(NX, dtype=jnp.int32) // 2
    row_table = jnp.stack([jnp.zeros((NX,), jnp.int32), jnp.full((NX,), NY - 1, jnp.int32)])
    column_table = jnp.stack([columns, columns])
    return jnp.stack([row_table, column_table], axis=1).astype(jnp.int32)


def plant(entries, own_key, smallest, largest):
    shape = entries.shape
    spot = [jax.random.randint(jax.random.fold_in(own_key, axis), (), 0, shape[axis]) for axis in range(len(shape))]
    entries = entries.at[tuple(spot)].set(smallest)
    longest = shape.index(max(shape))
    spot[longest] = (spot[longest] + 1) % shape[longest]
    return entries.at[tuple(spot)].set(largest)


def shard_levels(own_key, dims, cuts, smallest, high):
    def one(dim, blocks):
        steps = jax.random.uniform(jax.random.fold_in(jax.random.fold_in(own_key, 6), dim), (blocks,), jnp.float32, smallest / len(cuts), high / len(cuts))
        return jnp.repeat(jnp.exp(steps), dims[dim] // blocks).reshape((-1,) + (1,) * (len(dims) - dim - 1))

    gain = one(*cuts[0])
    for cut in cuts[1:]:
        gain = gain * one(*cut)
    return gain


def gaussian(own_key, dims, width, most, cuts=(), kind=jnp.bfloat16):
    loudness = shard_levels(own_key, dims, cuts, -0.22, 0.18) if cuts else 1.0
    entries = jax.random.normal(own_key, dims, jnp.float32) * width * loudness
    return jnp.minimum(jnp.maximum(entries, -most), most).astype(kind)


def setup_inputs(seed: int = 0) -> dict:
    arg_keys = jax.random.split(jax.random.key(seed), 9)
    elevation = gaussian(arg_keys[0], (2, NY, NX), 1.0, 6.0, ((0, 2), (1, 16)), jnp.float32)
    momentum_x = gaussian(arg_keys[1], (2, NY, NX), 1.0, 6.0, ((0, 2), (1, 16)), jnp.float32)
    momentum_y = gaussian(arg_keys[2], (2, NY, NX), 1.0, 6.0, ((0, 2), (1, 16)), jnp.float32)
    depth = jnp.clip(jnp.exp(math.log(1.0) - 1.609438 * jax.random.uniform(arg_keys[3], (2, NY, NX), jnp.float32) ** shard_levels(arg_keys[3], (2, NY, NX), ((0, 2), (1, 16)), -0.2, 0.2)), 0.2, 1.0)
    wet_mask = plant((jax.random.randint(arg_keys[4], (2, NY, NX), 0, 8) < 7).astype(jnp.int32), jax.random.fold_in(arg_keys[4], 1), 0, 1)
    inverse_x = draw_inverse_x(jax.random.fold_in(arg_keys[8], 71), 0)
    inverse_y = draw_inverse_y(jax.random.fold_in(arg_keys[8], 71), 0)
    nest_map = draw_nest_map(jax.random.fold_in(arg_keys[8], 71), 0)
    return {"elevation": elevation, "momentum_x": momentum_x, "momentum_y": momentum_y, "depth": depth, "wet_mask": wet_mask, "inverse_x": inverse_x, "inverse_y": inverse_y, "nest_map": nest_map}


step_ratio = 0.5
dispersion = 0.5
nest_blend = 0.5


def operate_last(field, coef):
    widths_right = [(0, 0)] * (field.ndim - 1) + [(0, 1)]
    widths_left = [(0, 0)] * (field.ndim - 1) + [(1, 0)]
    right = jnp.pad(field[..., 1:], widths_right)
    left = jnp.pad(field[..., :-1], widths_left)
    coef_left = jnp.pad(coef[..., :-1], widths_left)
    return field + coef * (field - right) + coef_left * (field - left)


def operate_rows(field, coef):
    flipped = operate_last(jnp.swapaxes(field, -1, -2), jnp.swapaxes(coef, -1, -2))
    return jnp.swapaxes(flipped, -1, -2)


def apply_columns(field, tables):
    split = field.reshape(2, NY, NX // GROUP, GROUP)
    result = jnp.einsum("skij,sykj->syki", tables, split, precision=lax.Precision.HIGHEST, preferred_element_type=jnp.float32)
    return result.reshape(2, NY, NX)


def apply_lines(field, tables):
    split = field.reshape(2, NY // GROUP, GROUP, NX)
    result = jnp.einsum("skij,skjx->skix", tables, split, precision=lax.Precision.HIGHEST, preferred_element_type=jnp.float32)
    return result.reshape(2, NY, NX)


def reference(elevation, momentum_x, momentum_y, depth, wet_mask, inverse_x, inverse_y, nest_map):
    wetness = wet_mask.astype(jnp.float32)
    face_x = wetness[:, :, :-1] * wetness[:, :, 1:] * (0.5 * (depth[:, :, :-1] + depth[:, :, 1:]))
    face_x = jnp.pad(face_x, ((0, 0), (0, 0), (0, 1)))
    face_y = wetness[:, :-1, :] * wetness[:, 1:, :] * (0.5 * (depth[:, :-1, :] + depth[:, 1:, :]))
    face_y = jnp.pad(face_y, ((0, 0), (0, 1), (0, 0)))
    coef_x = dispersion * face_x * face_x
    coef_y = dispersion * face_y * face_y
    height = elevation
    flow_x = momentum_x
    flow_y = momentum_y
    for step in range(STEPS):
        east = jnp.pad(height[:, :, 1:], ((0, 0), (0, 0), (0, 1)))
        south = jnp.pad(height[:, 1:, :], ((0, 0), (0, 1), (0, 0)))
        push_x = flow_x + step_ratio * face_x * (east - height)
        push_y = flow_y + step_ratio * face_y * (south - height)
        first_x = apply_columns(push_x, inverse_x)
        flow_x = first_x + apply_columns(push_x - operate_last(first_x, coef_x), inverse_x)
        first_y = apply_lines(push_y, inverse_y)
        flow_y = first_y + apply_lines(push_y - operate_rows(first_y, coef_y), inverse_y)
        flux_x = face_x * flow_x
        flux_y = face_y * flow_y
        west = jnp.pad(flux_x[:, :, :-1], ((0, 0), (0, 0), (1, 0)))
        north = jnp.pad(flux_y[:, :-1, :], ((0, 0), (1, 0), (0, 0)))
        height = height + step_ratio * (flux_x - west + flux_y - north)
        packet = height[0][nest_map[:, 0, :], nest_map[:, 1, :]]
        first_row = nest_blend * height[1, 0] + (1.0 - nest_blend) * packet[0]
        last_row = nest_blend * height[1, NY - 1] + (1.0 - nest_blend) * packet[1]
        height = height.at[1, 0].set(first_row)
        height = height.at[1, NY - 1].set(last_row)
    return (height, flow_x, flow_y)
```

```python
import jax
import jax.numpy as jnp
from jax import lax
from jax.experimental import pallas as pl
from jax.experimental.pallas import tpu as pltpu
from jax.sharding import PartitionSpec as P

LINE = ("rows", "sub")
VM = pl.BlockSpec(memory_space=pltpu.VMEM)
SM = pl.BlockSpec(memory_space=pltpu.SMEM)
F32 = jnp.float32


def moved(value, target):
    blocks = lax.axis_size("rows")
    pairs = []
    for source in range(2 * blocks):
        there = target(source // 2, source % 2)
        if there is not None and 0 <= there[0] < blocks:
            pairs.append((source, 2 * there[0] + there[1]))
    return lax.ppermute(value, LINE, pairs)


def swap_halves(value):
    return lax.ppermute(value, "sub", [(0, 1), (1, 0)])


def swap_nest(value):
    return lax.ppermute(value, "nest", [(0, 1), (1, 0)])


def call(body, outs, ins, scratch=(), flops=0):
    nbytes = sum(x.size * 4 for x in ins) + sum(4 * a * b for a, b in outs)
    return pl.pallas_call(
        body,
        out_shape=[jax.ShapeDtypeStruct(shape, F32) for shape in outs],
        in_specs=[SM if x.dtype == jnp.int32 and x.size < 16 else VM for x in ins],
        out_specs=[VM] * len(outs),
        scratch_shapes=list(scratch),
        cost_estimate=pl.CostEstimate(flops=flops, bytes_accessed=nbytes, transcendentals=0),
        compiler_params=pltpu.CompilerParams(vmem_limit_bytes=32 * 2**20),
    )(*ins)


def face_of(a, b):
    return jnp.where(jnp.logical_and(a > 0.0, b > 0.0), 0.5 * (a + b), 0.0)


def split(a):
    high = a.astype(jnp.bfloat16)
    low = (a - high.astype(F32)).astype(jnp.bfloat16)
    return high, low


def matmul(a, b):
    return jnp.dot(a, b, precision=lax.Precision.HIGHEST, preferred_element_type=F32)


def matmul_t(a, b):
    return lax.dot_general(
        a, b, (((1,), (1,)), ((), ())), precision=lax.Precision.HIGHEST, preferred_element_type=F32
    )


def row_iota(shape):
    return lax.broadcasted_iota(jnp.int32, shape, 0)


def next_row(x, edge):
    n = x.shape[0]
    return jnp.where(row_iota(x.shape) == n - 1, edge, pltpu.roll(x, n - 1, 0))


def prev_row(x, edge):
    return jnp.where(row_iota(x.shape) == 0, edge, pltpu.roll(x, 1, 0))


def prepare_body(h_ref, my_ref, depth_ref, wet_ref, buf_ref, edge_ref):
    n = h_ref.shape[0]
    h = h_ref[...]
    wd = depth_ref[...] * wet_ref[...].astype(F32)
    face = face_of(wd, next_row(wd, 0.0))
    buf_ref[0:n] = my_ref[...] + 0.5 * face * (next_row(h, 0.0) - h)
    buf_ref[n : 2 * n] = wd
    edge = jnp.concatenate([h[0:1], h[n - 1 : n], wd[0:1], wd[n - 1 : n], jnp.zeros((4, h.shape[1]), F32)], 0)
    buf_ref[2 * n : 2 * n + 8] = edge
    edge_ref[...] = edge


def across_body(h_ref, mx_ref, buf_ref, table_ref, flow_ref, hx_ref, push_ref, first_ref):
    n, width = h_ref.shape
    group = table_ref.shape[-1]
    h = h_ref[...]
    wd = buf_ref[n : 2 * n]
    lane = lax.broadcasted_iota(jnp.int32, wd.shape, 1)
    face = face_of(wd, jnp.where(lane == width - 1, 0.0, pltpu.roll(wd, width - 1, 1)))
    coef = 0.5 * face * face
    push = mx_ref[...] + 0.5 * face * (pltpu.roll(h, width - 1, 1) - h)
    push_ref[...] = push
    for b in range(width // group):
        cols = slice(b * group, (b + 1) * group)
        first_ref[:, cols] = matmul_t(push_ref[:, cols], table_ref[b])
    first = first_ref[...]
    operated = (
        first
        + coef * (first - pltpu.roll(first, width - 1, 1))
        + pltpu.roll(coef, 1, 1) * (first - pltpu.roll(first, 1, 1))
    )
    push_ref[...] = push - operated
    for b in range(width // group):
        cols = slice(b * group, (b + 1) * group)
        flow_ref[:, cols] = first_ref[:, cols] + matmul_t(push_ref[:, cols], table_ref[b])
    flux = face * flow_ref[...]
    hx_ref[...] = h + 0.5 * (flux - pltpu.roll(flux, 1, 1))


def solve_lines(push, face, face_above, table):
    coef = 0.5 * face * face
    coef_above = 0.5 * face_above * face_above
    first = matmul(table, push)
    operated = (
        first
        + coef * (first - next_row(first, 0.0))
        + prev_row(coef, coef_above) * (first - prev_row(first, 0.0))
    )
    flow = first + matmul(table, push - operated)
    g = push.shape[0]
    t_up = coef_above * first[0:1]
    u_down = coef[g - 1 : g] * first[g - 1 : g]
    return flow, t_up, u_down


def messages(flow, face, t_up, u_down, table, is_first):
    g = flow.shape[0]
    half_top = 0.5 * face[0:1]
    bottom = face[g - 1 : g]
    side = 0.5 * face[g - 2 : g - 1]
    rows = [
        t_up,
        half_top * flow[0:1],
        half_top * table[0:1, g - 1 : g],
        half_top * table[0:1, 0:1],
        u_down,
        bottom * flow[g - 1 : g],
        bottom * table[g - 1 : g, g - 1 : g],
        bottom * table[g - 1 : g, 0:1],
    ]
    nest_base = jnp.where(is_first, rows[1], -(side * flow[g - 2 : g - 1]))
    nest_coef = jnp.where(is_first, rows[2], -(side * table[g - 2 : g - 1, 0:1]))
    return jnp.concatenate(rows, 0), jnp.concatenate([nest_base, nest_coef], 0)


def lines_body(own_ref, other_ref, cross_ref, along_ref, table_ref, flow_ref, face_ref, msg_ref, nest_ref, aux_ref, push_ref, wd_ref):
    g = table_ref.shape[0]
    n = g // 2
    half = lax.axis_index("sub")
    lower = half == 0
    is_first = lax.axis_index("rows") == 0
    mine = pl.multiple_of(half * n, n)
    theirs = pl.multiple_of((1 - half) * n, n)
    push_ref[pl.ds(mine, n)] = own_ref[0:n]
    push_ref[pl.ds(theirs, n)] = other_ref[0:n]
    wd_ref[pl.ds(mine, n)] = own_ref[n : 2 * n]
    wd_ref[pl.ds(theirs, n)] = other_ref[n : 2 * n]
    own = own_ref[2 * n : 2 * n + 8]
    other = other_ref[2 * n : 2 * n + 8]
    cross = cross_ref[...]
    along = along_ref[...]
    top = jnp.where(lower, own, other)
    bottom = jnp.where(lower, other, own)
    below = jnp.where(lower, along, cross)
    above = jnp.where(lower, cross, along)
    wd = wd_ref[...]
    face = face_of(wd, next_row(wd, below[2:3]))
    face_above = face_of(above[3:4], wd[0:1])
    south = jnp.where(
        row_iota(wd.shape) == n - 1,
        0.5 * face * (bottom[0:1] - top[1:2]),
        jnp.where(row_iota(wd.shape) == g - 1, 0.5 * face * (below[0:1] - bottom[1:2]), 0.0),
    )
    table = table_ref[...]
    flow, t_up, u_down = solve_lines(push_ref[...] + south, face, face_above, table)
    flow_ref[...] = flow
    face_ref[...] = face
    msg_ref[...], nest_rows = messages(flow, face, t_up, u_down, table, is_first)
    nest_ref[0:2] = nest_rows
    nest_ref[2:8] = jnp.zeros((6, face.shape[1]), F32)
    aux_ref[...] = jnp.broadcast_to(face_above, aux_ref.shape)


def upsampled(row, base):
    width = row.shape[1]
    rolled = pltpu.roll(jnp.broadcast_to(row, (8, width)), lax.rem(width - base, width), 1)
    source = lax.broadcasted_iota(jnp.int32, (128, 256), 0)
    target = lax.broadcasted_iota(jnp.int32, (128, 256), 1)
    pick = jnp.where(target // 2 == source, 1.0, 0.0).astype(F32)
    pieces = [matmul(rolled[:, 128 * m : 128 * (m + 1)], pick) for m in range(width // 256)]
    return jnp.concatenate(pieces, 1)[0:1]


def neighbours(even_ref, odd_ref):
    is_even = lax.rem(lax.axis_index("rows"), 2) == 0
    even = even_ref[...]
    odd = odd_ref[...]
    return jnp.where(is_even, odd, even), jnp.where(is_even, even, odd)


def between_body(
    base_ref, flow_ref, face_ref, msg_ref, aux_ref, even_ref, odd_ref, even2_ref, odd2_ref, own_hx_ref, other_hx_ref,
    nest_row_ref, table_ref, h_ref, next_flow_ref, next_msg_ref, next_nest_ref, hx_ref,
):
    g = table_ref.shape[0]
    n = g // 2
    half = lax.axis_index("sub")
    block = lax.axis_index("rows")
    is_first = block == 0
    is_last = block == lax.axis_size("rows") - 1
    nearfield = lax.axis_index("nest") == 1
    mine = pl.multiple_of(half * n, n)
    theirs = pl.multiple_of((1 - half) * n, n)
    hx_ref[pl.ds(mine, n)] = own_hx_ref[...]
    hx_ref[pl.ds(theirs, n)] = other_hx_ref[...]
    own = msg_ref[...]
    above, below = neighbours(even_ref, odd_ref)
    low = lax.rem(block, 4) < 2
    above2 = jnp.where(low, odd2_ref[...], even2_ref[...])
    below2 = jnp.where(low, even2_ref[...], odd2_ref[...])
    table = table_ref[...]
    face = face_ref[...]
    t_row = below[0:1]
    u_row = above[4:5]
    flow = flow_ref[...] + table[:, g - 1 : g] * t_row + table[:, 0:1] * u_row
    flux = face * flow
    flux_above = above[5:6] + above[6:7] * own[0:1] + above[7:8] * above2[4:5]
    h_below = below[1:2] + below[2:3] * below2[0:1] + below[3:4] * own[4:5] - 0.5 * flux[g - 1 : g]
    h = hx_ref[...] + 0.5 * (flux - prev_row(flux, flux_above))
    packet = upsampled(nest_row_ref[0:1], base_ref[0])
    rows = row_iota(h.shape)
    blend = jnp.logical_and(
        nearfield,
        jnp.logical_or(jnp.logical_and(is_first, rows == 0), jnp.logical_and(is_last, rows == g - 1)),
    )
    h = jnp.where(blend, 0.5 * h + 0.5 * packet, h)
    hx_ref[...] = h
    h_ref[...] = hx_ref[pl.ds(mine, n)]
    push = flow + 0.5 * face * (next_row(h, h_below) - h)
    next_flow, t_up, u_down = solve_lines(push, face, aux_ref[0:1], table)
    next_flow_ref[...] = next_flow
    next_msg_ref[...], nest_rows = messages(next_flow, face, t_up, u_down, table, is_first)
    next_nest_ref[0:2] = nest_rows
    next_nest_ref[2:8] = jnp.zeros((6, face.shape[1]), F32)


def finish_body(
    base_ref, flow_ref, face_ref, msg_ref, even_ref, odd_ref, above2_ref, hx_ref, nest_row_ref, table_ref,
    h_ref, my_ref, flux_ref,
):
    g = table_ref.shape[0]
    n = g // 2
    half = lax.axis_index("sub")
    block = lax.axis_index("rows")
    is_first = jnp.logical_and(block == 0, half == 0)
    is_last = jnp.logical_and(block == lax.axis_size("rows") - 1, half == 1)
    nearfield = lax.axis_index("nest") == 1
    mine = pl.multiple_of(half * n, n)
    own = msg_ref[...]
    above, below = neighbours(even_ref, odd_ref)
    table = table_ref[...]
    flow = flow_ref[...] + table[:, g - 1 : g] * below[0:1] + table[:, 0:1] * above[4:5]
    flux = face_ref[...] * flow
    flux_above = above[5:6] + above[6:7] * own[0:1] + above[7:8] * above2_ref[4:5]
    flux_ref[0] = flow
    flux_ref[1] = flux - prev_row(flux, flux_above)
    my_ref[...] = flux_ref[0, pl.ds(mine, n)]
    h = hx_ref[...] + 0.5 * flux_ref[1, pl.ds(mine, n)]
    packet = upsampled(nest_row_ref[0:1], base_ref[0])
    rows = row_iota(h.shape)
    blend = jnp.logical_and(
        nearfield,
        jnp.logical_or(jnp.logical_and(is_first, rows == 0), jnp.logical_and(is_last, rows == n - 1)),
    )
    h_ref[...] = jnp.where(blend, 0.5 * h + 0.5 * packet, h)


def on_device(elevation, momentum_x, momentum_y, depth, wet_mask, inverse_x, inverse_y, nest_map):
    n, width = elevation.shape[1:]
    g = inverse_y.shape[-1]
    assert g == 2 * n and lax.axis_size("sub") == 2
    block = lax.axis_index("rows")
    half = lax.axis_index("sub")
    base = nest_map[0, 1, 0:1]
    height = elevation[0]
    table_x = inverse_x[0]
    table_y = lax.dynamic_index_in_dim(inverse_y[0], block, 0, keepdims=False)
    is_first = block == 0
    solve_flops = 2 * g * g * width * 2

    buf, edge = call(prepare_body, [(2 * n + 8, width), (8, width)], [height, momentum_y[0], depth[0], wet_mask[0]])
    other = swap_halves(buf)
    cross = moved(edge, lambda k, s: (k + 1, 0) if s == 1 else (k - 1, 1))
    along = moved(edge, lambda k, s: (k + 1, 1) if s == 1 else (k - 1, 0))
    flow_x, hx = call(
        across_body, [(n, width)] * 2, [height, momentum_x[0], buf, table_x],
        [pltpu.VMEM((n, width), F32)] * 2, solve_flops,
    )
    hx_edge = jnp.concatenate([hx[0:1], hx[n - 1 : n]], 0)
    other_edge = swap_halves(hx_edge)
    other_hx = swap_halves(hx)
    hx_top = jnp.where(half == 0, hx_edge[0:1], other_edge[0:1])
    hx_bottom = jnp.where(half == 0, other_edge[1:2], hx_edge[1:2])
    flow, face, msg, nest_rows, aux = call(
        lines_body, [(g, width), (g, width), (8, width), (8, width), (8, width)],
        [buf, other, cross, along, table_y], [pltpu.VMEM((g, width), F32)] * 2, solve_flops,
    )
    msg = jnp.concatenate([msg[0:1], msg[1:2] + hx_top, msg[2:]], 0)
    even = moved(msg, lambda k, s: (k ^ 1, s))
    odd = moved(msg, lambda k, s: (((k + 1) ^ 1) - 1, s))
    even2 = moved(msg, lambda k, s: (k ^ 2, s))
    odd2 = moved(msg, lambda k, s: (((k + 2) ^ 2) - 2, s))
    nest_row = nest_rows[0:1] + jnp.where(is_first, hx_top, hx_bottom) + nest_rows[1:2] * jnp.where(is_first, even[0:1], even[4:5])
    nest_row = swap_nest(nest_row)
    height, flow, msg, nest_rows = call(
        between_body, [(n, width), (g, width), (8, width), (8, width)],
        [base, flow, face, msg, aux, even, odd, even2, odd2, hx, other_hx, nest_row, table_y],
        [pltpu.VMEM((g, width), F32)], solve_flops,
    )
    even = moved(msg, lambda k, s: (k ^ 1, s))
    odd = moved(msg, lambda k, s: (((k + 1) ^ 1) - 1, s))
    above2 = moved(msg, lambda k, s: (k + 2, s))
    flow_x, hx = call(
        across_body, [(n, width)] * 2, [height, flow_x, buf, table_x],
        [pltpu.VMEM((n, width), F32)] * 2, solve_flops,
    )
    nest_row = (
        nest_rows[0:1] + jnp.where(half == 0, hx[0:1], hx[n - 1 : n])
        + nest_rows[1:2] * jnp.where(is_first, even[0:1], even[4:5])
    )
    nest_row = swap_nest(nest_row)
    height, flow_y = call(
        finish_body, [(n, width), (n, width)],
        [base, flow, face, msg, even, odd, above2, hx, nest_row, table_y],
        [pltpu.VMEM((2, g, width), F32)],
    )
    return height[None], flow_x[None], flow_y[None]


def solution(mesh):
    fields = P("nest", LINE, None)
    tables = P("nest", None, None, None)
    return jax.shard_map(
        on_device,
        mesh=mesh,
        in_specs=(fields,) * 5 + (tables, tables, P()),
        out_specs=(fields,) * 3,
        check_vma=False,
    )
```

```python
import jax
import jax.numpy as jnp
from jax import lax
from jax.experimental import pallas as pl
from jax.experimental.pallas import tpu as pltpu
from jax.sharding import PartitionSpec as P

LINE = ("rows", "sub")
VM = pl.BlockSpec(memory_space=pltpu.VMEM)
SM = pl.BlockSpec(memory_space=pltpu.SMEM)
FAR = pl.BlockSpec(memory_space=pltpu.HBM)
F32 = jnp.float32


def moved(value, target):
    blocks = lax.axis_size("rows")
    pairs = []
    for source in range(2 * blocks):
        there = target(source // 2, source % 2)
        if there is not None and 0 <= there[0] < blocks:
            pairs.append((source, 2 * there[0] + there[1]))
    return lax.ppermute(value, LINE, pairs)


def swap_halves(value):
    return lax.ppermute(value, "sub", [(0, 1), (1, 0)])


def swap_nest(value):
    return lax.ppermute(value, "nest", [(0, 1), (1, 0)])


def call(body, outs, ins, scratch=(), flops=0, far=(), far_outs=(), vmem=8):
    shapes = [o if isinstance(o, jax.ShapeDtypeStruct) else jax.ShapeDtypeStruct(o, F32) for o in outs]
    nbytes = sum(4 * x.size for i, x in enumerate(ins) if i not in far) + sum(4 * x.size for x in shapes)

    def spec(i, x, others):
        if i in others:
            return FAR
        return SM if x.dtype == jnp.int32 and x.size < 16 else VM

    return pl.pallas_call(
        body,
        out_shape=shapes,
        in_specs=[spec(i, x, far) for i, x in enumerate(ins)],
        out_specs=[spec(i, x, far_outs) for i, x in enumerate(shapes)],
        scratch_shapes=list(scratch),
        cost_estimate=pl.CostEstimate(flops=flops, bytes_accessed=nbytes, transcendentals=0),
        compiler_params=pltpu.CompilerParams(vmem_limit_bytes=vmem * 2**20),
    )(*ins)


def face_of(a, b):
    return jnp.where(jnp.logical_and(a > 0.0, b > 0.0), 0.5 * (a + b), 0.0)


def split(a):
    high = a.astype(jnp.bfloat16)
    low = (a - high.astype(F32)).astype(jnp.bfloat16)
    return high, low


def matmul(a, b):
    a_high, a_low = split(a)
    b_high, b_low = split(b)
    return jnp.dot(
        jnp.concatenate([a_high, a_high, a_low], 1),
        jnp.concatenate([b_high, b_low, b_high], 0),
        preferred_element_type=F32,
    )


def matmul_t(a, b):
    a_high, a_low = split(a)
    b_high, b_low = split(b)
    return lax.dot_general(
        jnp.concatenate([a_high, a_high, a_low], 1),
        jnp.concatenate([b_high, b_low, b_high], 1),
        (((1,), (1,)), ((), ())),
        preferred_element_type=F32,
    )


def row_iota(shape):
    return lax.broadcasted_iota(jnp.int32, shape, 0)


def next_row(x, edge):
    n = x.shape[0]
    return jnp.where(row_iota(x.shape) == n - 1, edge, pltpu.roll(x, n - 1, 0))


def prev_row(x, edge):
    return jnp.where(row_iota(x.shape) == 0, edge, pltpu.roll(x, 1, 0))


def prepare_body(h_far, my_far, depth_far, wet_far, buf_ref, edge_ref, h_ref, my_ref, depth_ref, wet_ref, sems):
    copies = [
        pltpu.make_async_copy(depth_far, depth_ref, sems.at[0]),
        pltpu.make_async_copy(wet_far, wet_ref, sems.at[1]),
        pltpu.make_async_copy(h_far, h_ref, sems.at[2]),
        pltpu.make_async_copy(my_far, my_ref, sems.at[3]),
    ]
    for copy in copies:
        copy.start()
    n = h_ref.shape[0]
    copies[0].wait()
    copies[1].wait()
    wd = depth_ref[...] * wet_ref[...].astype(F32)
    buf_ref[n : 2 * n] = wd
    face = face_of(wd, next_row(wd, 0.0))
    copies[2].wait()
    h = h_ref[...]
    edge = jnp.concatenate([h[0:1], h[n - 1 : n], wd[0:1], wd[n - 1 : n], jnp.zeros((4, h.shape[1]), F32)], 0)
    buf_ref[2 * n : 2 * n + 8] = edge
    edge_ref[...] = edge
    copies[3].wait()
    buf_ref[0:n] = my_ref[...] + 0.5 * face * (next_row(h, 0.0) - h)


def across(h_ref, mx_ref, buf_ref, table_ref, flow_ref, hx_ref, push_ref, first_ref):
    n, width = h_ref.shape
    group = table_ref.shape[-1]
    h = h_ref[...]
    wd = buf_ref[n : 2 * n]
    lane = lax.broadcasted_iota(jnp.int32, wd.shape, 1)
    face = face_of(wd, jnp.where(lane == width - 1, 0.0, pltpu.roll(wd, width - 1, 1)))
    coef = 0.5 * face * face
    push = mx_ref[...] + 0.5 * face * (pltpu.roll(h, width - 1, 1) - h)
    push_ref[...] = push
    for b in range(width // group):
        cols = slice(b * group, (b + 1) * group)
        first_ref[:, cols] = matmul_t(push_ref[:, cols], table_ref[b])
    first = first_ref[...]
    operated = (
        first
        + coef * (first - pltpu.roll(first, width - 1, 1))
        + pltpu.roll(coef, 1, 1) * (first - pltpu.roll(first, 1, 1))
    )
    push_ref[...] = push - operated
    for b in range(width // group):
        cols = slice(b * group, (b + 1) * group)
        flow_ref[:, cols] = first_ref[:, cols] + matmul_t(push_ref[:, cols], table_ref[b])
    flux = face * flow_ref[...]
    hx_ref[...] = h + 0.5 * (flux - pltpu.roll(flux, 1, 1))


def across_first_body(
    h_ref, mx_ref, buf_ref, table_ref, tables_far, map_far, along_ref,
    flow_ref, hx_ref, hx_edge_ref, line_table_ref, base_ref, push_ref, first_ref, map_ref, sems,
):
    n = h_ref.shape[0]
    fetch_table = pltpu.make_async_copy(tables_far.at[lax.axis_index("rows")], line_table_ref, sems.at[0])
    fetch_map = pltpu.make_async_copy(map_far.at[0, :, pl.ds(0, 128)], map_ref, sems.at[1])
    fetch_table.start()
    fetch_map.start()
    across(h_ref, mx_ref, buf_ref, table_ref, flow_ref, hx_ref, push_ref, first_ref)
    hx_edge_ref[0:1] = hx_ref[0:1]
    hx_edge_ref[1:2] = hx_ref[n - 1 : n]
    hx_edge_ref[2:8] = jnp.zeros((6, h_ref.shape[1]), F32)
    fetch_map.wait()
    base_ref[0] = map_ref[1, 0]
    fetch_table.wait()


def across_last_body(
    h_ref, mx_ref, buf_ref, table_ref, nest_ref, even_ref, flow_far, hx_ref, nest_row_ref, flow_ref, push_ref, first_ref, sem
):
    n = h_ref.shape[0]
    across(h_ref, mx_ref, buf_ref, table_ref, flow_ref, hx_ref, push_ref, first_ref)
    out = pltpu.make_async_copy(flow_ref, flow_far, sem)
    out.start()
    edge = jnp.where(lax.axis_index("sub") == 0, hx_ref[0:1], hx_ref[n - 1 : n])
    even = even_ref[...]
    row = nest_ref[0:1] + edge + nest_ref[1:2] * nest_factor(even)
    nest_row_ref[...] = jnp.broadcast_to(row, nest_row_ref.shape)
    out.wait()


def nest_factor(even):
    return jnp.where(lax.axis_index("rows") == 0, even[0:1], even[4:5])


def solve_lines(push, face, face_above, table):
    coef = 0.5 * face * face
    coef_above = 0.5 * face_above * face_above
    first = matmul(table, push)
    operated = (
        first
        + coef * (first - next_row(first, 0.0))
        + prev_row(coef, coef_above) * (first - prev_row(first, 0.0))
    )
    flow = first + matmul(table, push - operated)
    g = push.shape[0]
    t_up = coef_above * first[0:1]
    u_down = coef[g - 1 : g] * first[g - 1 : g]
    return flow, t_up, u_down


def messages(flow, face, t_up, u_down, table, is_first):
    g = flow.shape[0]
    half_top = 0.5 * face[0:1]
    bottom = face[g - 1 : g]
    side = 0.5 * face[g - 2 : g - 1]
    rows = [
        t_up,
        half_top * flow[0:1],
        half_top * table[0:1, g - 1 : g],
        half_top * table[0:1, 0:1],
        u_down,
        bottom * flow[g - 1 : g],
        bottom * table[g - 1 : g, g - 1 : g],
        bottom * table[g - 1 : g, 0:1],
    ]
    nest_base = jnp.where(is_first, rows[1], -(side * flow[g - 2 : g - 1]))
    nest_coef = jnp.where(is_first, rows[2], -(side * table[g - 2 : g - 1, 0:1]))
    return jnp.concatenate(rows, 0), jnp.concatenate([nest_base, nest_coef], 0)


def lines_body(
    own_ref, other_ref, cross_ref, along_ref, hx_ref, other_hx_ref, table_ref,
    flow_ref, face_ref, msg_ref, nest_ref, push_ref, wd_ref,
):
    g = table_ref.shape[0]
    n = g // 2
    half = lax.axis_index("sub")
    lower = half == 0
    is_first = lax.axis_index("rows") == 0
    mine = pl.multiple_of(half * n, n)
    theirs = pl.multiple_of((1 - half) * n, n)
    push_ref[pl.ds(mine, n)] = own_ref[0:n]
    push_ref[pl.ds(theirs, n)] = other_ref[0:n]
    wd_ref[pl.ds(mine, n)] = own_ref[n : 2 * n]
    wd_ref[pl.ds(theirs, n)] = other_ref[n : 2 * n]
    own = own_ref[2 * n : 2 * n + 8]
    other = other_ref[2 * n : 2 * n + 8]
    cross = cross_ref[...]
    along = along_ref[...]
    top = jnp.where(lower, own, other)
    bottom = jnp.where(lower, other, own)
    below = jnp.where(lower, along, cross)
    above = jnp.where(lower, cross, along)
    wd = wd_ref[...]
    face = face_of(wd, next_row(wd, below[2:3]))
    face_above = face_of(above[3:4], wd[0:1])
    south = jnp.where(
        row_iota(wd.shape) == n - 1,
        0.5 * face * (bottom[0:1] - top[1:2]),
        jnp.where(row_iota(wd.shape) == g - 1, 0.5 * face * (below[0:1] - bottom[1:2]), 0.0),
    )
    table = table_ref[...]
    flow, t_up, u_down = solve_lines(push_ref[...] + south, face, face_above, table)
    flow_ref[...] = flow
    face_ref[...] = face
    hx_top = jnp.where(lower, hx_ref[0:1], other_hx_ref[0:1])
    hx_bottom = jnp.where(lower, other_hx_ref[1:2], hx_ref[1:2])
    rows, nest_rows = messages(flow, face, t_up, u_down, table, is_first)
    msg_ref[...] = rows
    msg_ref[1:2] = rows[1:2] + hx_top
    nest_ref[0:1] = nest_rows[0:1] + jnp.where(is_first, hx_top, hx_bottom)
    nest_ref[1:2] = nest_rows[1:2]
    nest_ref[2:3] = face_above
    nest_ref[3:8] = jnp.zeros((5, face.shape[1]), F32)


def upsampled(row, base):
    width = row.shape[1]
    rolled = pltpu.roll(jnp.broadcast_to(row, (8, width)), lax.rem(width - base, width), 1)
    high = rolled.astype(jnp.bfloat16)
    middle, low = split(rolled - high.astype(F32))
    part = lax.broadcasted_iota(jnp.int32, rolled.shape, 0)
    parts = jnp.where(
        part == 0,
        high.astype(F32),
        jnp.where(part == 1, middle.astype(F32), jnp.where(part == 2, low.astype(F32), 0.0)),
    ).astype(jnp.bfloat16)
    source = lax.broadcasted_iota(jnp.int32, (128, 256), 0)
    target = lax.broadcasted_iota(jnp.int32, (128, 256), 1)
    pick = jnp.where(target // 2 == source, 1.0, 0.0).astype(jnp.bfloat16)
    pieces = [
        jnp.dot(parts[:, 128 * m : 128 * (m + 1)], pick, preferred_element_type=F32) for m in range(width // 256)
    ]
    picked = jnp.concatenate(pieces, 1)
    return picked[0:1] + picked[1:2] + picked[2:3]


def neighbours(even_ref, odd_ref):
    is_even = lax.rem(lax.axis_index("rows"), 2) == 0
    even = even_ref[...]
    odd = odd_ref[...]
    return jnp.where(is_even, odd, even), jnp.where(is_even, even, odd)


def between_body(
    base_ref, flow_ref, face_ref, msg_ref, nest_ref, even_ref, even2_ref, odd2_ref, odd_ref, own_hx_ref, other_hx_ref,
    nest_there_ref, even_there_ref, table_ref, h_ref, next_flow_ref, next_msg_ref, next_nest_ref, hx_ref,
):
    g = table_ref.shape[0]
    n = g // 2
    half = lax.axis_index("sub")
    block = lax.axis_index("rows")
    is_first = block == 0
    is_last = block == lax.axis_size("rows") - 1
    nearfield = lax.axis_index("nest") == 1
    mine = pl.multiple_of(half * n, n)
    theirs = pl.multiple_of((1 - half) * n, n)
    hx_ref[pl.ds(mine, n)] = own_hx_ref[...]
    hx_ref[pl.ds(theirs, n)] = other_hx_ref[...]
    own = msg_ref[...]
    above, below = neighbours(even_ref, odd_ref)
    low = lax.rem(block, 4) < 2
    above2 = jnp.where(low, odd2_ref[...], even2_ref[...])
    below2 = jnp.where(low, even2_ref[...], odd2_ref[...])
    table = table_ref[...]
    face = face_ref[...]
    t_row = below[0:1]
    u_row = above[4:5]
    flow = flow_ref[...] + table[:, g - 1 : g] * t_row + table[:, 0:1] * u_row
    flux = face * flow
    flux_above = above[5:6] + above[6:7] * own[0:1] + above[7:8] * above2[4:5]
    h_below = below[1:2] + below[2:3] * below2[0:1] + below[3:4] * own[4:5] - 0.5 * flux[g - 1 : g]
    h = hx_ref[...] + 0.5 * (flux - prev_row(flux, flux_above))
    packet = upsampled(nest_there_ref[0:1] + nest_there_ref[1:2] * nest_factor(even_there_ref[...]), base_ref[0])
    rows = row_iota(h.shape)
    blend = jnp.logical_and(
        nearfield,
        jnp.logical_or(jnp.logical_and(is_first, rows == 0), jnp.logical_and(is_last, rows == g - 1)),
    )
    h = jnp.where(blend, 0.5 * h + 0.5 * packet, h)
    hx_ref[...] = h
    h_ref[...] = hx_ref[pl.ds(mine, n)]
    push = flow + 0.5 * face * (next_row(h, h_below) - h)
    next_flow, t_up, u_down = solve_lines(push, face, nest_ref[2:3], table)
    next_flow_ref[...] = next_flow
    next_msg_ref[...], nest_rows = messages(next_flow, face, t_up, u_down, table, is_first)
    next_nest_ref[0:2] = nest_rows
    next_nest_ref[2:8] = jnp.zeros((6, face.shape[1]), F32)


def finish_body(
    base_ref, flow_ref, face_ref, msg_ref, even_ref, above2_ref, odd_ref, hx_ref, nest_row_ref, table_ref,
    h_far, my_far, h_ref, my_ref, sems,
):
    g = table_ref.shape[0]
    n = g // 2
    half = lax.axis_index("sub")
    block = lax.axis_index("rows")
    is_first = jnp.logical_and(block == 0, half == 0)
    is_last = jnp.logical_and(block == lax.axis_size("rows") - 1, half == 1)
    nearfield = lax.axis_index("nest") == 1
    mine = pl.ds(pl.multiple_of(half * n, n), n)
    own = msg_ref[...]
    above, below = neighbours(even_ref, odd_ref)
    t_row = below[0:1]
    u_row = above[4:5]
    table = table_ref[mine]
    flow = flow_ref[mine] + table[:, g - 1 : g] * t_row + table[:, 0:1] * u_row
    my_ref[...] = flow
    copy_my = pltpu.make_async_copy(my_ref, my_far, sems.at[0])
    copy_my.start()
    flux_above = above[5:6] + above[6:7] * own[0:1] + above[7:8] * above2_ref[4:5]
    flow_mid = flow_ref[n - 1 : n] + table_ref[n - 1 : n, g - 1 : g] * t_row + table_ref[n - 1 : n, 0:1] * u_row
    before = jnp.where(half == 0, flux_above, face_ref[n - 1 : n] * flow_mid)
    flux = face_ref[mine] * flow
    h = hx_ref[...] + 0.5 * (flux - prev_row(flux, before))
    packet = upsampled(nest_row_ref[0:1], base_ref[0])
    rows = row_iota(h.shape)
    blend = jnp.logical_and(
        nearfield,
        jnp.logical_or(jnp.logical_and(is_first, rows == 0), jnp.logical_and(is_last, rows == n - 1)),
    )
    h_ref[...] = jnp.where(blend, 0.5 * h + 0.5 * packet, h)
    copy_h = pltpu.make_async_copy(h_ref, h_far, sems.at[1])
    copy_h.start()
    copy_my.wait()
    copy_h.wait()


def on_device(elevation, momentum_x, momentum_y, depth, wet_mask, inverse_x, inverse_y, nest_map):
    n, width = elevation.shape[1:]
    g = inverse_y.shape[-1]
    assert g == 2 * n and lax.axis_size("sub") == 2
    height = elevation[0]
    table_x = inverse_x[0]
    solve_flops = 2 * g * g * width * 2
    part = pltpu.VMEM((n, width), F32)
    dma = pltpu.SemaphoreType.DMA

    buf, edge = call(
        prepare_body, [(2 * n + 8, width), (8, width)], [height, momentum_y[0], depth[0], wet_mask[0]],
        [part, part, part, pltpu.VMEM((n, width), jnp.int32), dma((4,))], far=(0, 1, 2, 3), vmem=60,
    )
    other = swap_halves(buf)
    cross = moved(edge, lambda k, s: (k + 1, 0) if s == 1 else (k - 1, 1))
    along = moved(edge, lambda k, s: (k + 1, 1) if s == 1 else (k - 1, 0))
    flow_x, hx, hx_edge, table_y, base = call(
        across_first_body, [(n, width), (n, width), (8, width), (g, g), jax.ShapeDtypeStruct((1,), jnp.int32)],
        [height, momentum_x[0], buf, table_x, inverse_y[0], nest_map, along],
        [part, part, pltpu.SMEM((2, 128), jnp.int32), dma((2,))], solve_flops, far=(4, 5),
    )
    other_edge = swap_halves(hx_edge)
    flow, face, msg, nest = call(
        lines_body, [(g, width), (g, width), (8, width), (8, width)],
        [buf, other, cross, along, hx_edge, other_edge, table_y], [pltpu.VMEM((g, width), F32)] * 2, solve_flops,
    )
    hx, msg = lax.optimization_barrier((hx, msg))
    other_hx = swap_halves(hx)
    odd = moved(msg, lambda k, s: (((k + 1) ^ 1) - 1, s))
    even = moved(msg, lambda k, s: (k ^ 1, s))
    odd2 = moved(msg, lambda k, s: (((k + 2) ^ 2) - 2, s))
    even2 = moved(msg, lambda k, s: (k ^ 2, s))
    nest_there = swap_nest(nest)
    even_there = swap_nest(even)
    height, flow, msg, next_nest = call(
        between_body, [(n, width), (g, width), (8, width), (8, width)],
        [base, flow, face, msg, nest, even, even2, odd2, odd, hx, other_hx, nest_there, even_there, table_y],
        [pltpu.VMEM((g, width), F32)], solve_flops,
    )
    odd = moved(msg, lambda k, s: (((k + 1) ^ 1) - 1, s))
    even = moved(msg, lambda k, s: (k ^ 1, s))
    above2 = moved(msg, lambda k, s: (k + 2, s))
    flow_x, hx, nest_row = call(
        across_last_body, [(n, width), (n, width), (8, width)],
        [height, flow_x, buf, table_x, next_nest, even],
        [part, part, part, dma], solve_flops, far_outs=(0,),
    )
    nest_row = swap_nest(nest_row)
    height, flow_y = call(
        finish_body, [(n, width), (n, width)],
        [base, flow, face, msg, even, above2, odd, hx, nest_row, table_y],
        [part, part, dma((2,))], far_outs=(0, 1),
    )
    return height[None], flow_x[None], flow_y[None]


def solution(mesh):
    fields = P("nest", LINE, None)
    tables = P("nest", None, None, None)
    return jax.shard_map(
        on_device,
        mesh=mesh,
        in_specs=(fields,) * 5 + (tables, tables, P()),
        out_specs=(fields,) * 3,
        check_vma=False,
    )
```

```python
import jax
import jax.numpy as jnp
from jax import lax
from jax.experimental import pallas as pl
from jax.experimental.pallas import tpu as pltpu
from jax.sharding import PartitionSpec as P

LINE = ("rows", "sub")
VM = pl.BlockSpec(memory_space=pltpu.VMEM)
SM = pl.BlockSpec(memory_space=pltpu.SMEM)
FAR = pl.BlockSpec(memory_space=pltpu.HBM)
F32 = jnp.float32


def moved(value, target):
    blocks = lax.axis_size("rows")
    pairs = []
    for source in range(2 * blocks):
        there = target(source // 2, source % 2)
        if there is not None and 0 <= there[0] < blocks:
            pairs.append((source, 2 * there[0] + there[1]))
    return lax.ppermute(value, LINE, pairs)


def swap_halves(value):
    return lax.ppermute(value, "sub", [(0, 1), (1, 0)])


def swap_nest(value):
    return lax.ppermute(value, "nest", [(0, 1), (1, 0)])


def call(body, outs, ins, scratch=(), flops=0, far=(), far_outs=(), vmem=8):
    shapes = [o if isinstance(o, jax.ShapeDtypeStruct) else jax.ShapeDtypeStruct(o, F32) for o in outs]
    nbytes = sum(4 * x.size for i, x in enumerate(ins) if i not in far) + sum(4 * x.size for x in shapes)

    def spec(i, x, others):
        if i in others:
            return FAR
        return SM if x.dtype == jnp.int32 and x.size < 16 else VM

    return pl.pallas_call(
        body,
        out_shape=shapes,
        in_specs=[spec(i, x, far) for i, x in enumerate(ins)],
        out_specs=[spec(i, x, far_outs) for i, x in enumerate(shapes)],
        scratch_shapes=list(scratch),
        cost_estimate=pl.CostEstimate(flops=flops, bytes_accessed=nbytes, transcendentals=0),
        compiler_params=pltpu.CompilerParams(vmem_limit_bytes=vmem * 2**20),
    )(*[pltpu.with_memory_space_constraint(x, pltpu.HBM) if i in far else x for i, x in enumerate(ins)])


def face_of(a, b):
    return jnp.where(jnp.logical_and(a > 0.0, b > 0.0), 0.5 * (a + b), 0.0)


def split(a):
    high = a.astype(jnp.bfloat16)
    low = (a - high.astype(F32)).astype(jnp.bfloat16)
    return high, low


def matmul(a, b):
    a_high, a_low = split(a)
    b_high, b_low = split(b)
    return jnp.dot(
        jnp.concatenate([a_high, a_high, a_low], 1),
        jnp.concatenate([b_high, b_low, b_high], 0),
        preferred_element_type=F32,
    )


def matmul_t(a, b):
    a_high, a_low = split(a)
    b_high, b_low = split(b)
    return lax.dot_general(
        jnp.concatenate([a_high, a_high, a_low], 1),
        jnp.concatenate([b_high, b_low, b_high], 1),
        (((1,), (1,)), ((), ())),
        preferred_element_type=F32,
    )


def row_iota(shape):
    return lax.broadcasted_iota(jnp.int32, shape, 0)


def next_row(x, edge):
    n = x.shape[0]
    return jnp.where(row_iota(x.shape) == n - 1, edge, pltpu.roll(x, n - 1, 0))


def prev_row(x, edge):
    return jnp.where(row_iota(x.shape) == 0, edge, pltpu.roll(x, 1, 0))


def prepare_body(
    h_far, my_far, depth_far, wet_far, mx_far, buf_ref, edge_ref, h_ref, mx_ref, my_ref, depth_ref, wet_ref, sems
):
    n, width = h_ref.shape
    parts = 4
    step = n // parts
    fetched = []
    for i, (far, near) in enumerate(
        [(depth_far, depth_ref), (wet_far, wet_ref), (h_far, h_ref), (my_far, my_ref), (mx_far, mx_ref)]
    ):
        copies = [
            pltpu.make_async_copy(far.at[pl.ds(p * step, step)], near.at[pl.ds(p * step, step)], sems.at[i, p])
            for p in range(parts)
        ]
        for copy in copies:
            copy.start()
        fetched.append(copies)

    def wait(i):
        for copy in fetched[i]:
            copy.wait()

    wait(0)
    wait(1)
    wd = depth_ref[...] * wet_ref[...].astype(F32)
    buf_ref[n : 2 * n] = wd
    face = face_of(wd, next_row(wd, 0.0))
    wait(2)
    h = h_ref[...]
    buf_ref[2 * n : 2 * n + 8] = jnp.concatenate([h[0:1], h[n - 1 : n], jnp.zeros((6, width), F32)], 0)
    wait(3)
    buf_ref[0:n] = my_ref[...] + 0.5 * face * (next_row(h, 0.0) - h)
    wait(4)
    edge_ref[...] = jnp.concatenate([h[0:1], wd[0:1], wd[n - 1 : n], mx_ref[0:1]], 0)


def across(h_ref, mx_ref, buf_ref, table_ref, flow_ref, hx_ref, push_ref, first_ref):
    n, width = h_ref.shape
    group = table_ref.shape[-1]
    h = h_ref[...]
    wd = buf_ref[n : 2 * n]
    lane = lax.broadcasted_iota(jnp.int32, wd.shape, 1)
    face = face_of(wd, jnp.where(lane == width - 1, 0.0, pltpu.roll(wd, width - 1, 1)))
    coef = 0.5 * face * face
    push = mx_ref[...] + 0.5 * face * (pltpu.roll(h, width - 1, 1) - h)
    push_ref[...] = push
    for b in range(width // group):
        cols = slice(b * group, (b + 1) * group)
        first_ref[:, cols] = matmul_t(push_ref[:, cols], table_ref[b])
    first = first_ref[...]
    operated = (
        first
        + coef * (first - pltpu.roll(first, width - 1, 1))
        + pltpu.roll(coef, 1, 1) * (first - pltpu.roll(first, 1, 1))
    )
    push_ref[...] = push - operated
    for b in range(width // group):
        cols = slice(b * group, (b + 1) * group)
        flow_ref[:, cols] = first_ref[:, cols] + matmul_t(push_ref[:, cols], table_ref[b])
    flux = face * flow_ref[...]
    hx_ref[...] = h + 0.5 * (flux - pltpu.roll(flux, 1, 1))


def across_first_body(
    h_ref, mx_ref, buf_ref, table_ref, tables_far, along_ref, flow_ref, hx_ref, line_table_ref, push_ref, first_ref, sem
):
    fetch_table = pltpu.make_async_copy(tables_far.at[lax.axis_index("rows")], line_table_ref, sem)
    fetch_table.start()
    across(h_ref, mx_ref, buf_ref, table_ref, flow_ref, hx_ref, push_ref, first_ref)
    fetch_table.wait()


def across_below_body(cross_ref, along_ref, table_ref, hx_ref, h_ref, mx_ref, wd_ref, flow_ref, push_ref, first_ref):
    below = jnp.where(lax.axis_index("sub") == 0, along_ref[...], cross_ref[...])
    h_ref[...] = jnp.broadcast_to(below[0:1], h_ref.shape)
    wd_ref[8:16] = jnp.broadcast_to(below[1:2], h_ref.shape)
    mx_ref[...] = jnp.broadcast_to(below[3:4], h_ref.shape)
    across(h_ref, mx_ref, wd_ref, table_ref, flow_ref, hx_ref, push_ref, first_ref)


def across_last_body(h_ref, mx_ref, buf_ref, table_ref, flow_far, hx_ref, flow_ref, push_ref, first_ref, sem):
    across(h_ref, mx_ref, buf_ref, table_ref, flow_ref, hx_ref, push_ref, first_ref)
    out = pltpu.make_async_copy(flow_ref, flow_far, sem)
    out.start()
    out.wait()


def relay_body(msg_ref, even_ref, both_ref):
    both_ref[0:8] = msg_ref[...]
    both_ref[8:16] = even_ref[...]


def packet_body(nest_ref, even_ref, map_ref, hx_ref, *refs):
    packet_ref = refs[-1]
    n = hx_ref.shape[0]
    lower = lax.axis_index("sub") == 0
    is_first = lax.axis_index("rows") == 0
    top = hx_ref[0:1]
    bottom = hx_ref[n - 1 : n]
    for other_ref in refs[:-1]:
        top, bottom = jnp.where(lower, top, other_ref[0:1]), jnp.where(lower, other_ref[n - 1 : n], bottom)
    row = jnp.where(is_first, top, bottom) + nest_ref[0:1] + nest_ref[1:2] * nest_factor(even_ref[...])
    base = jnp.min(map_ref[0, 1:2, 0:128].astype(F32)).astype(jnp.int32)
    packet_ref[...] = jnp.broadcast_to(upsampled(row, base), packet_ref.shape)


def nest_factor(even):
    return jnp.where(lax.axis_index("rows") == 0, even[0:1], even[4:5])


def solve_lines(push, face, face_above, table):
    coef = 0.5 * face * face
    coef_above = 0.5 * face_above * face_above
    first = matmul(table, push)
    operated = (
        first
        + coef * (first - next_row(first, 0.0))
        + prev_row(coef, coef_above) * (first - prev_row(first, 0.0))
    )
    flow = first + matmul(table, push - operated)
    g = push.shape[0]
    t_up = coef_above * first[0:1]
    u_down = coef[g - 1 : g] * first[g - 1 : g]
    return flow, t_up, u_down


def messages(flow, face, t_up, u_down, table, is_first):
    g = flow.shape[0]
    half_top = 0.5 * face[0:1]
    bottom = face[g - 1 : g]
    side = 0.5 * face[g - 2 : g - 1]
    rows = [
        t_up,
        half_top * flow[0:1],
        half_top * table[0:1, g - 1 : g],
        half_top * table[0:1, 0:1],
        u_down,
        bottom * flow[g - 1 : g],
        bottom * table[g - 1 : g, g - 1 : g],
        bottom * table[g - 1 : g, 0:1],
    ]
    nest_base = jnp.where(is_first, rows[1], -(side * flow[g - 2 : g - 1]))
    nest_coef = jnp.where(is_first, rows[2], -(side * table[g - 2 : g - 1, 0:1]))
    return jnp.concatenate(rows, 0), jnp.concatenate([nest_base, nest_coef], 0)


def lines_body(
    own_ref, other_ref, cross_ref, along_ref, table_ref,
    flow_ref, face_ref, msg_ref, nest_ref, push_ref, wd_ref,
):
    g = table_ref.shape[0]
    n = g // 2
    half = lax.axis_index("sub")
    lower = half == 0
    is_first = lax.axis_index("rows") == 0
    mine = pl.multiple_of(half * n, n)
    theirs = pl.multiple_of((1 - half) * n, n)
    push_ref[pl.ds(mine, n)] = own_ref[0:n]
    push_ref[pl.ds(theirs, n)] = other_ref[0:n]
    wd_ref[pl.ds(mine, n)] = own_ref[n : 2 * n]
    wd_ref[pl.ds(theirs, n)] = other_ref[n : 2 * n]
    own = own_ref[2 * n : 2 * n + 8]
    other = other_ref[2 * n : 2 * n + 8]
    cross = cross_ref[...]
    along = along_ref[...]
    top = jnp.where(lower, own, other)
    bottom = jnp.where(lower, other, own)
    below = jnp.where(lower, along, cross)
    above = jnp.where(lower, cross, along)
    wd = wd_ref[...]
    face = face_of(wd, next_row(wd, below[1:2]))
    face_above = face_of(above[2:3], wd[0:1])
    south = jnp.where(
        row_iota(wd.shape) == n - 1,
        0.5 * face * (bottom[0:1] - top[1:2]),
        jnp.where(row_iota(wd.shape) == g - 1, 0.5 * face * (below[0:1] - bottom[1:2]), 0.0),
    )
    table = table_ref[...]
    flow, t_up, u_down = solve_lines(push_ref[...] + south, face, face_above, table)
    flow_ref[...] = flow
    face_ref[...] = face
    rows, nest_rows = messages(flow, face, t_up, u_down, table, is_first)
    msg_ref[...] = rows
    nest_ref[0:1] = nest_rows[0:1]
    nest_ref[1:2] = nest_rows[1:2]
    nest_ref[2:3] = face_above
    nest_ref[3:8] = jnp.zeros((5, face.shape[1]), F32)


def upsampled(row, base):
    width = row.shape[1]
    rolled = pltpu.roll(jnp.broadcast_to(row, (8, width)), lax.rem(width - base, width), 1)
    high = rolled.astype(jnp.bfloat16)
    middle, low = split(rolled - high.astype(F32))
    part = lax.broadcasted_iota(jnp.int32, rolled.shape, 0)
    parts = jnp.where(
        part == 0,
        high.astype(F32),
        jnp.where(part == 1, middle.astype(F32), jnp.where(part == 2, low.astype(F32), 0.0)),
    ).astype(jnp.bfloat16)
    source = lax.broadcasted_iota(jnp.int32, (128, 256), 0)
    target = lax.broadcasted_iota(jnp.int32, (128, 256), 1)
    pick = jnp.where(target // 2 == source, 1.0, 0.0).astype(jnp.bfloat16)
    pieces = [
        jnp.dot(parts[:, 128 * m : 128 * (m + 1)], pick, preferred_element_type=F32) for m in range(width // 256)
    ]
    picked = jnp.concatenate(pieces, 1)
    return picked[0:1] + picked[1:2] + picked[2:3]


def neighbours(even_ref, even2_ref, odd2_ref):
    block = lax.axis_index("rows")
    is_even = lax.rem(block, 2) == 0
    is_low = lax.rem(block, 4) < 2
    even = even_ref[...]
    even2 = even2_ref[...]
    odd2 = odd2_ref[...]
    up = jnp.where(is_low, odd2, even2)
    down = jnp.where(is_low, even2, odd2)
    return jnp.where(is_even, up[8:16], even), jnp.where(is_even, even, down[8:16]), up[0:8], down[0:8]


def between_body(
    flow_ref, face_ref, msg_ref, nest_ref, even_ref, even2_ref, odd2_ref, own_hx_ref, other_hx_ref,
    hx_below_ref, packet_ref, table_ref, h_ref, next_flow_ref, next_msg_ref, next_nest_ref, hx_ref,
):
    g = table_ref.shape[0]
    n = g // 2
    half = lax.axis_index("sub")
    block = lax.axis_index("rows")
    is_first = block == 0
    is_last = block == lax.axis_size("rows") - 1
    nearfield = lax.axis_index("nest") == 1
    mine = pl.multiple_of(half * n, n)
    theirs = pl.multiple_of((1 - half) * n, n)
    hx_ref[pl.ds(mine, n)] = own_hx_ref[...]
    hx_ref[pl.ds(theirs, n)] = other_hx_ref[...]
    own = msg_ref[...]
    above, below, above2, below2 = neighbours(even_ref, even2_ref, odd2_ref)
    table = table_ref[...]
    face = face_ref[...]
    t_row = below[0:1]
    u_row = above[4:5]
    flow = flow_ref[...] + table[:, g - 1 : g] * t_row + table[:, 0:1] * u_row
    flux = face * flow
    flux_above = above[5:6] + above[6:7] * own[0:1] + above[7:8] * above2[4:5]
    h_below = hx_below_ref[0:1] + below[1:2] + below[2:3] * below2[0:1] + below[3:4] * own[4:5] - 0.5 * flux[g - 1 : g]
    h = hx_ref[...] + 0.5 * (flux - prev_row(flux, flux_above))
    packet = packet_ref[0:1]
    rows = row_iota(h.shape)
    blend = jnp.logical_and(
        nearfield,
        jnp.logical_or(jnp.logical_and(is_first, rows == 0), jnp.logical_and(is_last, rows == g - 1)),
    )
    h = jnp.where(blend, 0.5 * h + 0.5 * packet, h)
    hx_ref[...] = h
    h_ref[...] = hx_ref[pl.ds(mine, n)]
    push = flow + 0.5 * face * (next_row(h, h_below) - h)
    next_flow, t_up, u_down = solve_lines(push, face, nest_ref[2:3], table)
    next_flow_ref[...] = next_flow
    next_msg_ref[...], nest_rows = messages(next_flow, face, t_up, u_down, table, is_first)
    next_nest_ref[0:2] = nest_rows
    next_nest_ref[2:8] = jnp.zeros((6, face.shape[1]), F32)


def finish_body(
    flow_ref, face_ref, msg_ref, even_ref, above2_ref, odd_ref, hx_ref, packet_ref, table_ref,
    h_far, my_far, h_ref, my_ref, sems,
):
    g = table_ref.shape[0]
    n = g // 2
    half = lax.axis_index("sub")
    block = lax.axis_index("rows")
    is_first = jnp.logical_and(block == 0, half == 0)
    is_last = jnp.logical_and(block == lax.axis_size("rows") - 1, half == 1)
    nearfield = lax.axis_index("nest") == 1
    mine = pl.ds(pl.multiple_of(half * n, n), n)
    own = msg_ref[...]
    is_even = lax.rem(block, 2) == 0
    above = jnp.where(is_even, odd_ref[...], even_ref[...])
    below = jnp.where(is_even, even_ref[...], odd_ref[...])
    t_row = below[0:1]
    u_row = above[4:5]
    table = table_ref[mine]
    flow = flow_ref[mine] + table[:, g - 1 : g] * t_row + table[:, 0:1] * u_row
    my_ref[...] = flow
    copy_my = pltpu.make_async_copy(my_ref, my_far, sems.at[0])
    copy_my.start()
    flux_above = above[5:6] + above[6:7] * own[0:1] + above[7:8] * above2_ref[4:5]
    flow_mid = flow_ref[n - 1 : n] + table_ref[n - 1 : n, g - 1 : g] * t_row + table_ref[n - 1 : n, 0:1] * u_row
    before = jnp.where(half == 0, flux_above, face_ref[n - 1 : n] * flow_mid)
    flux = face_ref[mine] * flow
    h = hx_ref[...] + 0.5 * (flux - prev_row(flux, before))
    packet = packet_ref[0:1]
    rows = row_iota(h.shape)
    blend = jnp.logical_and(
        nearfield,
        jnp.logical_or(jnp.logical_and(is_first, rows == 0), jnp.logical_and(is_last, rows == n - 1)),
    )
    h_ref[...] = jnp.where(blend, 0.5 * h + 0.5 * packet, h)
    copy_h = pltpu.make_async_copy(h_ref, h_far, sems.at[1])
    copy_h.start()
    copy_my.wait()
    copy_h.wait()


def on_device(elevation, momentum_x, momentum_y, depth, wet_mask, inverse_x, inverse_y, nest_map):
    n, width = elevation.shape[1:]
    g = inverse_y.shape[-1]
    assert g == 2 * n and lax.axis_size("sub") == 2
    table_x = inverse_x[0]
    solve_flops = 2 * g * g * width * 2
    part = pltpu.VMEM((n, width), F32)
    slab = pltpu.VMEM((8, width), F32)
    dma = pltpu.SemaphoreType.DMA

    buf, edge, height, flow_x = call(
        prepare_body, [(g + 8, width), (4, width), (n, width), (n, width)],
        [elevation[0], momentum_y[0], depth[0], wet_mask[0], momentum_x[0]],
        [part, part, pltpu.VMEM((n, width), jnp.int32), dma((5, 4))], far=(0, 1, 2, 3, 4),
    )
    other = swap_halves(buf)
    cross = moved(edge, lambda k, s: (k + 1, 0) if s == 1 else (k - 1, 1))
    along = moved(edge, lambda k, s: (k + 1, 1) if s == 1 else (k - 1, 0))
    flow_x, hx, table_y = call(
        across_first_body, [(n, width), (n, width), (g, g)],
        [height, flow_x, buf, table_x, inverse_y[0], along], [part, part, dma], solve_flops, far=(4,),
    )
    other_hx = swap_halves(lax.optimization_barrier((hx, cross))[0])
    flow, face, msg, nest = call(
        lines_body, [(g, width), (g, width), (8, width), (8, width)],
        [buf, other, cross, along, table_y], [pltpu.VMEM((g, width), F32)] * 2, solve_flops,
    )
    even = moved(msg, lambda k, s: (k ^ 1, s))
    (both,) = call(relay_body, [(16, width)], [msg, even])
    even2 = moved(both, lambda k, s: (k ^ 2, s))
    odd2 = moved(both, lambda k, s: (((k + 2) ^ 2) - 2, s))
    (hx_below,) = call(
        across_below_body, [(8, width)], [cross, along, table_x], [slab, slab, pltpu.VMEM((16, width), F32)] + [slab] * 3
    )
    (packet,) = call(packet_body, [(8, width)], [nest, even, nest_map, hx, other_hx])
    packet = swap_nest(packet)
    height, flow, msg, nest = call(
        between_body, [(n, width), (g, width), (8, width), (8, width)],
        [flow, face, msg, nest, even, even2, odd2, hx, other_hx, hx_below, packet, table_y],
        [pltpu.VMEM((g, width), F32)], solve_flops,
    )
    even = moved(msg, lambda k, s: (k ^ 1, s))
    odd = moved(msg, lambda k, s: (((k + 1) ^ 1) - 1, s))
    above2 = moved(msg, lambda k, s: (k + 2, s) if s == 0 else None)
    flow_x, hx = call(
        across_last_body, [(n, width), (n, width)],
        [height, flow_x, buf, table_x],
        [part, part, part, dma], solve_flops, far_outs=(0,),
    )
    (packet,) = call(packet_body, [(8, width)], [nest, even, nest_map, hx])
    packet = swap_nest(packet)
    height, flow_y = call(
        finish_body, [(n, width), (n, width)],
        [flow, face, msg, even, above2, odd, hx, packet, table_y],
        [part, part, dma((2,))], far_outs=(0, 1),
    )
    return height[None], flow_x[None], flow_y[None]


def solution(mesh):
    fields = P("nest", LINE, None)
    tables = P("nest", None, None, None)
    return jax.shard_map(
        on_device,
        mesh=mesh,
        in_specs=(fields,) * 5 + (tables, tables, P()),
        out_specs=(fields,) * 3,
        check_vma=False,
    )
```

```python
import jax
import jax.numpy as jnp
from jax import lax
from jax.experimental import pallas as pl
from jax.experimental.pallas import tpu as pltpu
from jax.sharding import PartitionSpec as P

LINE = ("rows", "sub")
VM = pl.BlockSpec(memory_space=pltpu.VMEM)
SM = pl.BlockSpec(memory_space=pltpu.SMEM)
FAR = pl.BlockSpec(memory_space=pltpu.HBM)
F32 = jnp.float32


def moved(value, target):
    blocks = lax.axis_size("rows")
    pairs = []
    for source in range(2 * blocks):
        there = target(source // 2, source % 2)
        if there is not None and 0 <= there[0] < blocks:
            pairs.append((source, 2 * there[0] + there[1]))
    return lax.ppermute(value, LINE, pairs)


def swap_halves(value):
    return lax.ppermute(value, "sub", [(0, 1), (1, 0)])


def swap_nest(value):
    return lax.ppermute(value, "nest", [(0, 1), (1, 0)])


def call(body, outs, ins, scratch=(), flops=0, far=(), far_outs=(), vmem=8, aliases=None):
    shapes = [o if isinstance(o, jax.ShapeDtypeStruct) else jax.ShapeDtypeStruct(o, F32) for o in outs]
    nbytes = sum(4 * x.size for i, x in enumerate(ins) if i not in far) + sum(4 * x.size for x in shapes)

    def spec(i, x, others):
        if i in others:
            return FAR
        return SM if x.dtype == jnp.int32 and x.size < 16 else VM

    return pl.pallas_call(
        body,
        out_shape=shapes,
        in_specs=[spec(i, x, far) for i, x in enumerate(ins)],
        out_specs=[spec(i, x, far_outs) for i, x in enumerate(shapes)],
        scratch_shapes=list(scratch),
        input_output_aliases=aliases or {},
        cost_estimate=pl.CostEstimate(flops=flops, bytes_accessed=nbytes, transcendentals=0),
        compiler_params=pltpu.CompilerParams(vmem_limit_bytes=vmem * 2**20),
    )(*[pltpu.with_memory_space_constraint(x, pltpu.HBM) if i in far else x for i, x in enumerate(ins)])


def face_of(a, b):
    return jnp.where(jnp.logical_and(a > 0.0, b > 0.0), 0.5 * (a + b), 0.0)


def split(a):
    high = a.astype(jnp.bfloat16)
    low = (a - high.astype(F32)).astype(jnp.bfloat16)
    return high, low


def matmul(a, b):
    a_high, a_low = split(a)
    b_high, b_low = split(b)
    return jnp.dot(
        jnp.concatenate([a_high, a_high, a_low], 1),
        jnp.concatenate([b_high, b_low, b_high], 0),
        preferred_element_type=F32,
    )


def matmul_t(a, b):
    a_high, a_low = split(a)
    b_high, b_low = split(b)
    return lax.dot_general(
        jnp.concatenate([a_high, a_high, a_low], 1),
        jnp.concatenate([b_high, b_low, b_high], 1),
        (((1,), (1,)), ((), ())),
        preferred_element_type=F32,
    )


def row_iota(shape):
    return lax.broadcasted_iota(jnp.int32, shape, 0)


def next_row(x, edge):
    n = x.shape[0]
    return jnp.where(row_iota(x.shape) == n - 1, edge, pltpu.roll(x, n - 1, 0))


def prev_row(x, edge):
    return jnp.where(row_iota(x.shape) == 0, edge, pltpu.roll(x, 1, 0))


def copies_of(source, target, sems, parts=4):
    step = source.shape[0] // parts
    return [
        pltpu.make_async_copy(source.at[pl.ds(p * step, step)], target.at[pl.ds(p * step, step)], sems.at[p])
        for p in range(parts)
    ]


def depth_body(depth_far, wet_far, wd_ref, depth_ref, wet_ref, sems):
    copies = copies_of(depth_far, depth_ref, sems.at[0]) + copies_of(wet_far, wet_ref, sems.at[1])
    for copy in copies:
        copy.start()
    for copy in copies:
        copy.wait()
    wd_ref[...] = depth_ref[...] * wet_ref[...].astype(F32)


def prepare_body(h_far, my_far, mx_far, wd_ref, buf_ref, edge_ref, h_ref, mx_ref, my_ref, sems):
    n, width = h_ref.shape
    fetched = []
    for i, (far, near) in enumerate([(h_far, h_ref), (my_far, my_ref), (mx_far, mx_ref)]):
        fetched += copies_of(far, near, sems.at[i])
    for copy in fetched:
        copy.start()
    for copy in fetched:
        copy.wait()
    wd = wd_ref[...]
    h = h_ref[...]
    buf_ref[0:n] = my_ref[...] + 0.5 * face_of(wd, next_row(wd, 0.0)) * (next_row(h, 0.0) - h)
    buf_ref[n : n + 8] = jnp.concatenate([h[0:1], h[n - 1 : n], jnp.zeros((6, width), F32)], 0)
    edge_ref[...] = jnp.concatenate([h[0:1], wd[0:1], wd[n - 1 : n], mx_ref[0:1]], 0)


def across(h_ref, mx_ref, wd_ref, table_ref, flow_ref, hx_ref, push_ref, first_ref):
    n, width = h_ref.shape
    group = table_ref.shape[-1]
    h = h_ref[...]
    wd = wd_ref[...]
    lane = lax.broadcasted_iota(jnp.int32, wd.shape, 1)
    face = face_of(wd, jnp.where(lane == width - 1, 0.0, pltpu.roll(wd, width - 1, 1)))
    coef = 0.5 * face * face
    push = mx_ref[...] + 0.5 * face * (pltpu.roll(h, width - 1, 1) - h)
    push_ref[...] = push
    for b in range(width // group):
        cols = slice(b * group, (b + 1) * group)
        first_ref[:, cols] = matmul_t(push_ref[:, cols], table_ref[b])
    first = first_ref[...]
    operated = (
        first
        + coef * (first - pltpu.roll(first, width - 1, 1))
        + pltpu.roll(coef, 1, 1) * (first - pltpu.roll(first, 1, 1))
    )
    push_ref[...] = push - operated
    for b in range(width // group):
        cols = slice(b * group, (b + 1) * group)
        flow_ref[:, cols] = first_ref[:, cols] + matmul_t(push_ref[:, cols], table_ref[b])
    flux = face * flow_ref[...]
    hx_ref[...] = h + 0.5 * (flux - pltpu.roll(flux, 1, 1))


def across_first_body(
    h_ref, mx_ref, wd_ref, table_ref, tables_far, along_ref, flow_ref, hx_ref, line_table_ref, push_ref, first_ref, sem
):
    fetch_table = pltpu.make_async_copy(tables_far.at[lax.axis_index("rows")], line_table_ref, sem)
    fetch_table.start()
    across(h_ref, mx_ref, wd_ref, table_ref, flow_ref, hx_ref, push_ref, first_ref)
    fetch_table.wait()


def across_below_body(cross_ref, along_ref, table_ref, hx_ref, h_ref, mx_ref, wd_ref, flow_ref, push_ref, first_ref):
    below = jnp.where(lax.axis_index("sub") == 0, along_ref[...], cross_ref[...])
    h_ref[...] = jnp.broadcast_to(below[0:1], h_ref.shape)
    wd_ref[...] = jnp.broadcast_to(below[1:2], h_ref.shape)
    mx_ref[...] = jnp.broadcast_to(below[3:4], h_ref.shape)
    across(h_ref, mx_ref, wd_ref, table_ref, flow_ref, hx_ref, push_ref, first_ref)


def relay_body(msg_ref, even_ref, out_ref):
    is_even = lax.rem(lax.axis_index("rows"), 2) == 0
    even = even_ref[...]
    msg = msg_ref[...]
    passed = jnp.where(is_even, even[4:8], even[0:4])
    out_ref[...] = jnp.concatenate([msg[0:1], msg[4:5], passed, jnp.zeros((2, msg.shape[1]), F32)], 0)


def packet_body(nest_ref, even_ref, map_ref, hx_ref, other_ref, packet_ref):
    n = hx_ref.shape[0]
    lower = lax.axis_index("sub") == 0
    is_first = lax.axis_index("rows") == 0
    top = hx_ref[0:1]
    bottom = hx_ref[n - 1 : n]
    if other_ref.shape == hx_ref.shape:
        top, bottom = jnp.where(lower, top, other_ref[0:1]), jnp.where(lower, other_ref[n - 1 : n], bottom)
    row = jnp.where(is_first, top, bottom) + nest_ref[0:1] + nest_ref[1:2] * nest_factor(even_ref)
    base = jnp.min(map_ref[0, 1:2, 0:128].astype(F32)).astype(jnp.int32)
    packet_ref[...] = upsampled(row, base)


def nest_factor(even_ref):
    down = even_ref.shape[0] // 2
    if down == 2:
        down = 1
    return jnp.where(lax.axis_index("rows") == 0, even_ref[0:1], even_ref[down : down + 1])


def solve_lines(push, face, face_above, table):
    coef = 0.5 * face * face
    coef_above = 0.5 * face_above * face_above
    first = matmul(table, push)
    operated = (
        first
        + coef * (first - next_row(first, 0.0))
        + prev_row(coef, coef_above) * (first - prev_row(first, 0.0))
    )
    flow = first + matmul(table, push - operated)
    g = push.shape[0]
    t_up = coef_above * first[0:1]
    u_down = coef[g - 1 : g] * first[g - 1 : g]
    return flow, t_up, u_down


def messages(flow, face, t_up, u_down, table, is_first):
    g = flow.shape[0]
    half_top = 0.5 * face[0:1]
    bottom = face[g - 1 : g]
    side = 0.5 * face[g - 2 : g - 1]
    rows = [
        t_up,
        half_top * flow[0:1],
        half_top * table[0:1, g - 1 : g],
        half_top * table[0:1, 0:1],
        u_down,
        bottom * flow[g - 1 : g],
        bottom * table[g - 1 : g, g - 1 : g],
        bottom * table[g - 1 : g, 0:1],
    ]
    nest_base = jnp.where(is_first, rows[1], -(side * flow[g - 2 : g - 1]))
    nest_coef = jnp.where(is_first, rows[2], -(side * table[g - 2 : g - 1, 0:1]))
    return jnp.concatenate(rows, 0), jnp.concatenate([nest_base, nest_coef], 0)


def faces_body(own_wd_ref, other_wd_ref, face_ref, wd_ref):
    n = own_wd_ref.shape[0]
    half = lax.axis_index("sub")
    wd_ref[pl.ds(pl.multiple_of(half * n, n), n)] = own_wd_ref[...]
    wd_ref[pl.ds(pl.multiple_of((1 - half) * n, n), n)] = other_wd_ref[...]
    wd = wd_ref[...]
    face_ref[...] = face_of(wd, next_row(wd, 0.0))


def lines_body(
    own_ref, own_wd_ref, other_ref, other_wd_ref, cross_ref, along_ref, table_ref, inner_ref,
    flow_ref, face_ref, msg_ref, nest_ref, push_ref,
):
    g = table_ref.shape[0]
    n = g // 2
    half = lax.axis_index("sub")
    lower = half == 0
    is_first = lax.axis_index("rows") == 0
    mine = pl.multiple_of(half * n, n)
    theirs = pl.multiple_of((1 - half) * n, n)
    push_ref[pl.ds(mine, n)] = own_ref[0:n]
    push_ref[pl.ds(theirs, n)] = other_ref[0:n]
    own = own_ref[n : n + 8]
    other = other_ref[n : n + 8]
    cross = cross_ref[...]
    along = along_ref[...]
    top = jnp.where(lower, own, other)
    bottom = jnp.where(lower, other, own)
    below = jnp.where(lower, along, cross)
    above = jnp.where(lower, cross, along)
    face = inner_ref[...]
    wd_last = jnp.where(lower, other_wd_ref[n - 1 : n], own_wd_ref[n - 1 : n])
    face = jnp.where(row_iota(face.shape) == g - 1, face_of(wd_last, below[1:2]), face)
    face_above = face_of(above[2:3], jnp.where(lower, own_wd_ref[0:1], other_wd_ref[0:1]))
    south = jnp.where(
        row_iota(face.shape) == n - 1,
        0.5 * face * (bottom[0:1] - top[1:2]),
        jnp.where(row_iota(face.shape) == g - 1, 0.5 * face * (below[0:1] - bottom[1:2]), 0.0),
    )
    table = table_ref[...]
    flow, t_up, u_down = solve_lines(push_ref[...] + south, face, face_above, table)
    flow_ref[...] = flow
    face_ref[...] = face
    rows, nest_rows = messages(flow, face, t_up, u_down, table, is_first)
    msg_ref[...] = rows
    nest_ref[0:1] = nest_rows[0:1]
    nest_ref[1:2] = nest_rows[1:2]
    nest_ref[2:3] = face_above
    nest_ref[3:8] = jnp.zeros((5, face.shape[1]), F32)


def upsampled(row, base):
    width = row.shape[1]
    rolled = pltpu.roll(jnp.broadcast_to(row, (8, width)), lax.rem(width - base, width), 1)
    high = rolled.astype(jnp.bfloat16)
    middle, low = split(rolled - high.astype(F32))
    part = lax.broadcasted_iota(jnp.int32, rolled.shape, 0)
    parts = jnp.where(
        part == 0,
        high.astype(F32),
        jnp.where(part == 1, middle.astype(F32), jnp.where(part == 2, low.astype(F32), 0.0)),
    ).astype(jnp.bfloat16)
    source = lax.broadcasted_iota(jnp.int32, (128, 256), 0)
    target = lax.broadcasted_iota(jnp.int32, (128, 256), 1)
    pick = jnp.where(target // 2 == source, 1.0, 0.0).astype(jnp.bfloat16)
    pieces = [
        jnp.dot(parts[:, 128 * m : 128 * (m + 1)], pick, preferred_element_type=F32) for m in range(width // 256)
    ]
    picked = jnp.concatenate(pieces, 1)
    return picked[0:1] + picked[1:2] + picked[2:3]


def neighbours(even_ref, even2_ref, odd2_ref):
    block = lax.axis_index("rows")
    is_even = lax.rem(block, 2) == 0
    is_low = lax.rem(block, 4) < 2
    even = even_ref[...]
    even2 = even2_ref[...]
    odd2 = odd2_ref[...]
    up = jnp.where(is_low, odd2, even2)
    down = jnp.where(is_low, even2, odd2)
    return jnp.where(is_even, up[2:6], even[4:8]), jnp.where(is_even, even[0:4], down[2:6]), up[1:2], down[0:1]


def between_body(
    flow_ref, face_ref, msg_ref, nest_ref, even_ref, odd2_ref, even2_ref, own_hx_ref, other_hx_ref,
    hx_below_ref, packet_ref, table_ref, h_ref, next_flow_ref, next_msg_ref, next_nest_ref, gain_ref, u_down_ref, hx_ref,
):
    g = table_ref.shape[0]
    n = g // 2
    half = lax.axis_index("sub")
    block = lax.axis_index("rows")
    is_first = block == 0
    is_last = block == lax.axis_size("rows") - 1
    nearfield = lax.axis_index("nest") == 1
    mine = pl.multiple_of(half * n, n)
    theirs = pl.multiple_of((1 - half) * n, n)
    hx_ref[pl.ds(mine, n)] = own_hx_ref[...]
    hx_ref[pl.ds(theirs, n)] = other_hx_ref[...]
    own = msg_ref[...]
    above, below, u_above2, t_below2 = neighbours(even_ref, even2_ref, odd2_ref)
    table = table_ref[...]
    face = face_ref[...]
    t_row = below[0:1]
    u_row = above[0:1]
    flow = flow_ref[...] + table[:, g - 1 : g] * t_row + table[:, 0:1] * u_row
    flux = face * flow
    flux_above = above[1:2] + above[2:3] * own[0:1] + above[3:4] * u_above2
    h_below = hx_below_ref[0:1] + below[1:2] + below[2:3] * t_below2 + below[3:4] * own[4:5] - 0.5 * flux[g - 1 : g]
    h = hx_ref[...] + 0.5 * (flux - prev_row(flux, flux_above))
    packet = packet_ref[0:1]
    rows = row_iota(h.shape)
    blend = jnp.logical_and(
        nearfield,
        jnp.logical_or(jnp.logical_and(is_first, rows == 0), jnp.logical_and(is_last, rows == g - 1)),
    )
    h = jnp.where(blend, 0.5 * h + 0.5 * packet, h)
    hx_ref[...] = h
    h_ref[...] = hx_ref[pl.ds(mine, n)]
    push = flow + 0.5 * face * (next_row(h, h_below) - h)
    next_flow, t_up, u_down = solve_lines(push, face, nest_ref[2:3], table)
    next_flow_ref[...] = next_flow
    rows, nest_rows = messages(next_flow, face, t_up, u_down, table, is_first)
    next_msg_ref[...] = jnp.concatenate([t_up, u_down, rows[5:6], jnp.zeros_like(t_up)], 0)
    u_down_ref[...] = u_down
    gain_ref[0:2] = above[2:4]
    gain_ref[2:8] = jnp.zeros((6, t_up.shape[1]), F32)
    next_nest_ref[0:2] = nest_rows
    next_nest_ref[2:8] = jnp.zeros((6, face.shape[1]), F32)


def finish_body(
    flow_ref, even_ref, odd_ref, table_ref, face_ref, hx_ref, flow_x_ref,
    my_far, flow_x_far, h_far, edge_ref, before_ref, my_ref, h_ref, sems,
):
    copies = copies_of(flow_x_ref, flow_x_far, sems.at[0])
    for copy in copies:
        copy.start()
    g, width = flow_ref.shape
    n = g // 2
    half = lax.axis_index("sub")
    mine = pl.ds(pl.multiple_of(half * n, n), n)
    is_even = lax.rem(lax.axis_index("rows"), 2) == 0
    above = jnp.where(is_even, odd_ref[...], even_ref[...])
    below = jnp.where(is_even, even_ref[...], odd_ref[...])
    t_row = below[0:1]
    u_row = above[1:2]
    table = table_ref[mine]
    flow = flow_ref[mine] + table[:, g - 1 : g] * t_row + table[:, 0:1] * u_row
    my_ref[...] = flow
    for copy in copies_of(my_ref, my_far, sems.at[1]):
        copy.start()
        copies.append(copy)
    flux = face_ref[mine] * flow
    h_ref[...] = hx_ref[...] + 0.5 * (flux - prev_row(flux, 0.0))
    inner = pl.ds(8, n - 16)
    copies.append(pltpu.make_async_copy(h_ref.at[inner], h_far.at[inner], sems.at[2, 0]))
    copies[-1].start()
    edge_ref[0:8] = h_ref[0:8]
    edge_ref[8:16] = h_ref[n - 8 : n]
    flow_mid = flow_ref[n - 1 : n] + table_ref[n - 1 : n, g - 1 : g] * t_row + table_ref[n - 1 : n, 0:1] * u_row
    before_ref[0:1] = face_ref[n - 1 : n] * flow_mid
    before_ref[1:2] = above[2:3]
    before_ref[2:8] = jnp.zeros((6, width), F32)
    for copy in copies:
        copy.wait()


def finish_edge_body(h_in, edge_ref, before_ref, msg_ref, gain_ref, above2_ref, packet_ref, h_far, rows_ref, sems):
    n = h_far.shape[0]
    half = lax.axis_index("sub")
    block = lax.axis_index("rows")
    nearfield = lax.axis_index("nest") == 1
    is_first = jnp.logical_and(nearfield, jnp.logical_and(block == 0, half == 0))
    is_last = jnp.logical_and(nearfield, jnp.logical_and(block == lax.axis_size("rows") - 1, half == 1))
    flux_above = before_ref[1:2] + gain_ref[0:1] * msg_ref[0:1] + gain_ref[1:2] * above2_ref[...]
    before = jnp.where(half == 0, flux_above, before_ref[0:1])
    packet = packet_ref[...]
    edge = edge_ref[...]
    rows = row_iota(edge.shape)
    edge = jnp.where(rows == 0, edge - 0.5 * before, edge)
    blend = jnp.logical_or(jnp.logical_and(is_first, rows == 0), jnp.logical_and(is_last, rows == 15))
    rows_ref[...] = jnp.where(blend, 0.5 * edge + 0.5 * packet, edge)
    copies = [
        pltpu.make_async_copy(rows_ref.at[pl.ds(0, 8)], h_far.at[pl.ds(0, 8)], sems.at[0]),
        pltpu.make_async_copy(rows_ref.at[pl.ds(8, 8)], h_far.at[pl.ds(n - 8, 8)], sems.at[1]),
    ]
    for copy in copies:
        copy.start()
    for copy in copies:
        copy.wait()


def on_device(elevation, momentum_x, momentum_y, depth, wet_mask, inverse_x, inverse_y, nest_map):
    n, width = elevation.shape[1:]
    g = inverse_y.shape[-1]
    assert g == 2 * n and lax.axis_size("sub") == 2
    table_x = inverse_x[0]
    solve_flops = 2 * g * g * width * 2
    part = pltpu.VMEM((n, width), F32)
    slab = pltpu.VMEM((8, width), F32)
    dma = pltpu.SemaphoreType.DMA

    (wd,) = call(
        depth_body, [(n, width)], [depth[0], wet_mask[0]],
        [part, pltpu.VMEM((n, width), jnp.int32), dma((2, 4))], far=(0, 1),
    )
    other_wd = swap_halves(wd)
    buf, edge, height, flow_x = call(
        prepare_body, [(n + 8, width), (4, width), (n, width), (n, width)],
        [elevation[0], momentum_y[0], momentum_x[0], wd],
        [part, dma((3, 4))], far=(0, 1, 2), flops=int(0),
    )
    other = swap_halves(buf)
    cross = moved(edge, lambda k, s: (k + 1, 0) if s == 1 else (k - 1, 1))
    along = moved(edge, lambda k, s: (k + 1, 1) if s == 1 else (k - 1, 0))
    flow_x, hx, table_y = call(
        across_first_body, [(n, width), (n, width), (g, g)],
        [height, flow_x, wd, table_x, inverse_y[0], along], [part, part, dma], solve_flops, far=(4,),
    )
    (inner,) = call(faces_body, [(g, width)], [wd, other_wd], [pltpu.VMEM((g, width), F32)], flops=int(1e9))
    flow, face, msg, nest = call(
        lines_body, [(g, width), (g, width), (8, width), (8, width)],
        [buf, wd, other, other_wd, cross, along, table_y, inner], [pltpu.VMEM((g, width), F32)], solve_flops,
    )
    other_hx = swap_halves(lax.optimization_barrier((hx, msg))[0])
    even = moved(msg, lambda k, s: (k ^ 1, s))
    (both,) = call(relay_body, [(8, width)], [msg, even], flops=int(3e9))
    even2 = moved(both, lambda k, s: (k ^ 2, s))
    odd2 = moved(both, lambda k, s: (((k + 2) ^ 2) - 2, s))
    (hx_below,) = call(
        across_below_body, [(8, width)], [cross, along, table_x], [slab] * 6
    )
    (packet,) = call(packet_body, [(1, width)], [nest, even, nest_map, hx, other_hx])
    packet = swap_nest(packet)
    height, flow, msg, nest, gain, u_down = call(
        between_body, [(n, width), (g, width), (4, width), (8, width), (8, width), (1, width)],
        [flow, face, msg, nest, even, odd2, even2, hx, other_hx, hx_below, packet, table_y],
        [pltpu.VMEM((g, width), F32)], solve_flops,
    )
    even = moved(msg, lambda k, s: (k ^ 1, s))
    odd = moved(msg, lambda k, s: (((k + 1) ^ 1) - 1, s))
    above2 = moved(u_down, lambda k, s: (k + 2, s) if s == 0 else None)
    flow_x, hx = call(across, [(n, width), (n, width)], [height, flow_x, wd, table_x], [part, part], solve_flops)
    (packet,) = call(packet_body, [(1, width)], [nest, even, nest_map, hx, odd])
    packet = swap_nest(packet)
    flow_y, flow_x, height, edge, before = call(
        finish_body, [(n, width), (n, width), (n, width), (16, width), (8, width)],
        [flow, even, odd, table_y, face, hx, flow_x], [part, part, dma((3, 4))], far_outs=(0, 1, 2),
    )
    (height,) = call(
        finish_edge_body, [(n, width)], [height, edge, before, msg, gain, above2, packet],
        [pltpu.VMEM((16, width), F32), dma((2,))], far=(0,), far_outs=(0,), aliases={0: 0},
    )
    return height[None], flow_x[None], flow_y[None]


def solution(mesh):
    fields = P("nest", LINE, None)
    tables = P("nest", None, None, None)
    return jax.shard_map(
        on_device,
        mesh=mesh,
        in_specs=(fields,) * 5 + (tables, tables, P()),
        out_specs=(fields,) * 3,
        check_vma=False,
    )
```

```python
import jax
import jax.numpy as jnp
from jax import lax
from jax.experimental import pallas as pl
from jax.experimental.pallas import tpu as pltpu
from jax.sharding import PartitionSpec as P

LINE = ("rows", "sub")
VM = pl.BlockSpec(memory_space=pltpu.VMEM)
SM = pl.BlockSpec(memory_space=pltpu.SMEM)
FAR = pl.BlockSpec(memory_space=pltpu.HBM)
F32 = jnp.float32


def moved(value, target):
    blocks = lax.axis_size("rows")
    pairs = []
    for source in range(2 * blocks):
        there = target(source // 2, source % 2)
        if there is not None and 0 <= there[0] < blocks:
            pairs.append((source, 2 * there[0] + there[1]))
    return lax.ppermute(value, LINE, pairs)


def swap_halves(value):
    return lax.ppermute(value, "sub", [(0, 1), (1, 0)])


def swap_nest(value):
    return lax.ppermute(value, "nest", [(0, 1), (1, 0)])


def call(body, outs, ins, scratch=(), flops=0, far=(), far_outs=(), vmem=8, aliases=None):
    shapes = [o if isinstance(o, jax.ShapeDtypeStruct) else jax.ShapeDtypeStruct(o, F32) for o in outs]
    nbytes = sum(4 * x.size for i, x in enumerate(ins) if i not in far) + sum(4 * x.size for x in shapes)

    def spec(i, x, others):
        if i in others:
            return FAR
        return SM if x.dtype == jnp.int32 and x.size < 16 else VM

    return pl.pallas_call(
        body,
        out_shape=shapes,
        in_specs=[spec(i, x, far) for i, x in enumerate(ins)],
        out_specs=[spec(i, x, far_outs) for i, x in enumerate(shapes)],
        scratch_shapes=list(scratch),
        input_output_aliases=aliases or {},
        cost_estimate=pl.CostEstimate(flops=flops, bytes_accessed=nbytes, transcendentals=0),
        compiler_params=pltpu.CompilerParams(vmem_limit_bytes=vmem * 2**20),
    )(*[pltpu.with_memory_space_constraint(x, pltpu.HBM) if i in far else x for i, x in enumerate(ins)])


def by_columns(body, width, step):
    def run(*refs):
        for start in range(0, width, step):
            body(*[ref.at[:, pl.ds(start, step)] if ref.shape[-1] == width else ref for ref in refs])

    return run


def face_of(a, b):
    return jnp.where(jnp.logical_and(a > 0.0, b > 0.0), 0.5 * (a + b), 0.0)


def split(a):
    high = a.astype(jnp.bfloat16)
    low = (a - high.astype(F32)).astype(jnp.bfloat16)
    return high, low


def stacked(a):
    high, low = split(a)
    return jnp.concatenate([jnp.concatenate([high, high], 1), jnp.concatenate([low, jnp.zeros_like(low)], 1)], 0)


def folded(product):
    rows = product.shape[0] // 2
    return product[:rows] + product[rows:]


def matmul(a, b):
    return folded(jnp.dot(stacked(a), jnp.concatenate(split(b), 0), preferred_element_type=F32))


def matmul_t(a, b):
    wide = jnp.concatenate(split(b), 1)
    return folded(
        lax.dot_general(stacked(a), wide, (((1,), (1,)), ((), ())), preferred_element_type=F32)
    )


def row_iota(shape):
    return lax.broadcasted_iota(jnp.int32, shape, 0)


def next_row(x, edge):
    n = x.shape[0]
    return jnp.where(row_iota(x.shape) == n - 1, edge, pltpu.roll(x, n - 1, 0))


def prev_row(x, edge):
    return jnp.where(row_iota(x.shape) == 0, edge, pltpu.roll(x, 1, 0))


def copies_of(source, target, sems, parts=4):
    step = source.shape[0] // parts
    return [
        pltpu.make_async_copy(source.at[pl.ds(p * step, step)], target.at[pl.ds(p * step, step)], sems.at[p])
        for p in range(parts)
    ]


def depth_body(depth_far, wet_far, wd_ref, depth_ref, wet_ref, sems):
    copies = copies_of(depth_far, depth_ref, sems.at[0]) + copies_of(wet_far, wet_ref, sems.at[1])
    for copy in copies:
        copy.start()
    for copy in copies:
        copy.wait()
    wd_ref[...] = depth_ref[...] * wet_ref[...].astype(F32)


def prepare_body(h_far, my_far, mx_far, wd_ref, buf_ref, edge_ref, h_ref, mx_ref, my_ref, sems):
    n, width = h_ref.shape
    fetched = []
    for i, (far, near) in enumerate([(h_far, h_ref), (my_far, my_ref), (mx_far, mx_ref)]):
        fetched += copies_of(far, near, sems.at[i])
    for copy in fetched:
        copy.start()
    for copy in fetched:
        copy.wait()
    wd = wd_ref[...]
    h = h_ref[...]
    buf_ref[0:n] = my_ref[...] + 0.5 * face_of(wd, next_row(wd, 0.0)) * (next_row(h, 0.0) - h)
    buf_ref[n : n + 8] = jnp.concatenate([h[0:1], h[n - 1 : n], jnp.zeros((6, width), F32)], 0)
    outward = jnp.where(lax.axis_index("sub") == 0, wd[0:1], wd[n - 1 : n])
    edge_ref[...] = jnp.concatenate([h[0:1], outward, mx_ref[0:1], face_of(wd[0:1], wd[1:2])], 0)


def across(h_ref, mx_ref, wd_ref, table_ref, flow_ref, hx_ref, push_ref, first_ref):
    n, width = h_ref.shape
    group = table_ref.shape[-1]
    h = h_ref[...]
    wd = wd_ref[...]
    lane = lax.broadcasted_iota(jnp.int32, wd.shape, 1)
    face = face_of(wd, jnp.where(lane == width - 1, 0.0, pltpu.roll(wd, width - 1, 1)))
    coef = 0.5 * face * face
    push = mx_ref[...] + 0.5 * face * (pltpu.roll(h, width - 1, 1) - h)
    push_ref[...] = push
    for b in range(width // group):
        cols = slice(b * group, (b + 1) * group)
        first_ref[:, cols] = matmul_t(push_ref[:, cols], table_ref[b])
    first = first_ref[...]
    operated = (
        first
        + coef * (first - pltpu.roll(first, width - 1, 1))
        + pltpu.roll(coef, 1, 1) * (first - pltpu.roll(first, 1, 1))
    )
    push_ref[...] = push - operated
    for b in range(width // group):
        cols = slice(b * group, (b + 1) * group)
        flow_ref[:, cols] = first_ref[:, cols] + matmul_t(push_ref[:, cols], table_ref[b])
    flux = face * flow_ref[...]
    hx_ref[...] = h + 0.5 * (flux - pltpu.roll(flux, 1, 1))


def across_first_body(
    h_ref, mx_ref, wd_ref, table_ref, tables_far, along_ref,
    flow_ref, hx_ref, line_table_ref, near_tables_ref, push_ref, first_ref, sems,
):
    block = lax.axis_index("rows")
    group = line_table_ref.shape[0]
    up = jnp.maximum(block - 1, 0)
    down = jnp.minimum(block + 1, tables_far.shape[0] - 1)
    fetches = [
        pltpu.make_async_copy(tables_far.at[block], line_table_ref, sems.at[0]),
        pltpu.make_async_copy(tables_far.at[up, pl.ds(group - 8, 8)], near_tables_ref.at[pl.ds(0, 8)], sems.at[1]),
        pltpu.make_async_copy(tables_far.at[down, pl.ds(0, 8)], near_tables_ref.at[pl.ds(8, 8)], sems.at[2]),
    ]
    for fetch in fetches:
        fetch.start()
    across(h_ref, mx_ref, wd_ref, table_ref, flow_ref, hx_ref, push_ref, first_ref)
    for fetch in fetches:
        fetch.wait()


def across_below_body(cross_ref, along_ref, table_ref, hx_ref, h_ref, mx_ref, wd_ref, flow_ref, push_ref, first_ref):
    below = jnp.where(lax.axis_index("sub") == 0, along_ref[...], cross_ref[...])
    h_ref[...] = jnp.broadcast_to(below[0:1], h_ref.shape)
    wd_ref[...] = jnp.broadcast_to(below[1:2], h_ref.shape)
    mx_ref[...] = jnp.broadcast_to(below[2:3], h_ref.shape)
    across(h_ref, mx_ref, wd_ref, table_ref, flow_ref, hx_ref, push_ref, first_ref)


def relay_body(msg_ref, even_ref, out_ref):
    is_even = lax.rem(lax.axis_index("rows"), 2) == 0
    even = even_ref[...]
    msg = msg_ref[...]
    passed = jnp.where(is_even, even[2:4], even[0:2])
    out_ref[...] = jnp.concatenate([msg[0:1], msg[2:3], passed], 0)


def packet_body(nest_ref, even_ref, map_ref, hx_ref, other_ref, packet_ref):
    n = hx_ref.shape[0]
    lower = lax.axis_index("sub") == 0
    is_first = lax.axis_index("rows") == 0
    top = hx_ref[0:1]
    bottom = hx_ref[n - 1 : n]
    if other_ref.shape == hx_ref.shape:
        top, bottom = jnp.where(lower, top, other_ref[0:1]), jnp.where(lower, other_ref[n - 1 : n], bottom)
    row = jnp.where(is_first, top, bottom) + nest_ref[0:1] + nest_ref[1:2] * nest_factor(even_ref)
    base = jnp.min(map_ref[0, 1:2, 0:128].astype(F32)).astype(jnp.int32)
    packet_ref[...] = upsampled(row, base)


def nest_factor(even_ref):
    return jnp.where(lax.axis_index("rows") == 0, even_ref[0:1], even_ref[2:3])


def solve_lines(push, face, face_above, table):
    coef = 0.5 * face * face
    coef_above = 0.5 * face_above * face_above
    first = matmul(table, push)
    step = coef * (first - next_row(first, 0.0))
    flow = first + matmul(table, push - first - step + prev_row(step, -(coef_above * first[0:1])))
    g = push.shape[0]
    t_up = coef_above * first[0:1]
    u_down = coef[g - 1 : g] * first[g - 1 : g]
    return flow, t_up, u_down


def messages(flow, face, t_up, u_down, table, is_first):
    g = flow.shape[0]
    half_top = 0.5 * face[0:1]
    side = 0.5 * face[g - 2 : g - 1]
    rows = [t_up, half_top * flow[0:1], u_down, face[g - 1 : g] * flow[g - 1 : g]]
    nest_base = jnp.where(is_first, rows[1], -(side * flow[g - 2 : g - 1]))
    nest_coef = jnp.where(is_first, half_top * table[0:1, g - 1 : g], -(side * table[g - 2 : g - 1, 0:1]))
    return jnp.concatenate(rows, 0), jnp.concatenate([nest_base, nest_coef], 0)


def faces_body(own_wd_ref, other_wd_ref, face_ref, wd_ref):
    n = own_wd_ref.shape[0]
    half = lax.axis_index("sub")
    wd_ref[pl.ds(pl.multiple_of(half * n, n), n)] = own_wd_ref[...]
    wd_ref[pl.ds(pl.multiple_of((1 - half) * n, n), n)] = other_wd_ref[...]
    wd = wd_ref[...]
    face_ref[...] = face_of(wd, next_row(wd, 0.0))


def lines_body(
    own_ref, own_wd_ref, other_ref, other_wd_ref, cross_ref, along_ref, table_ref, near_tables_ref, inner_ref,
    flow_ref, face_ref, msg_ref, nest_ref, gain_ref, push_ref,
):
    g = table_ref.shape[0]
    n = g // 2
    half = lax.axis_index("sub")
    lower = half == 0
    is_first = lax.axis_index("rows") == 0
    mine = pl.multiple_of(half * n, n)
    theirs = pl.multiple_of((1 - half) * n, n)
    push_ref[pl.ds(mine, n)] = own_ref[0:n]
    push_ref[pl.ds(theirs, n)] = other_ref[0:n]
    own = own_ref[n : n + 8]
    other = other_ref[n : n + 8]
    cross = cross_ref[...]
    along = along_ref[...]
    top = jnp.where(lower, own, other)
    bottom = jnp.where(lower, other, own)
    below = jnp.where(lower, along, cross)
    above = jnp.where(lower, cross, along)
    wd_last = jnp.where(lower, other_wd_ref[n - 1 : n], own_wd_ref[n - 1 : n])
    face_ref[...] = inner_ref[...]
    face_ref[g - 1 : g] = face_of(wd_last, below[1:2])
    face_above = face_of(above[1:2], jnp.where(lower, own_wd_ref[0:1], other_wd_ref[0:1]))
    push_ref[n - 1 : n] += 0.5 * face_ref[n - 1 : n] * (bottom[0:1] - top[1:2])
    push_ref[g - 1 : g] += 0.5 * face_ref[g - 1 : g] * (below[0:1] - bottom[1:2])
    face = face_ref[...]
    table = table_ref[...]
    flow, t_up, u_down = solve_lines(push_ref[...], face, face_above, table)
    flow_ref[...] = flow
    rows, nest_rows = messages(flow, face, t_up, u_down, table, is_first)
    msg_ref[...] = rows
    nest_ref[0:1] = nest_rows[0:1]
    nest_ref[1:2] = nest_rows[1:2]
    half_below = 0.5 * below[3:4]
    near = near_tables_ref[...]
    gain_ref[0:1] = half_below * near[8:9, g - 1 : g]
    gain_ref[1:2] = half_below * near[8:9, 0:1]
    gain_ref[2:3] = face_above * near[7:8, g - 1 : g]
    gain_ref[3:4] = face_above * near[7:8, 0:1]
    gain_ref[4:8] = jnp.zeros((4, half_below.shape[1]), F32)
    nest_ref[2:3] = face_above
    nest_ref[3:8] = jnp.zeros((5, face.shape[1]), F32)


def upsampled(row, base):
    width = row.shape[1]
    rolled = pltpu.roll(jnp.broadcast_to(row, (8, width)), lax.rem(width - base, width), 1)
    high = rolled.astype(jnp.bfloat16)
    middle, low = split(rolled - high.astype(F32))
    part = lax.broadcasted_iota(jnp.int32, rolled.shape, 0)
    parts = jnp.where(
        part == 0,
        high.astype(F32),
        jnp.where(part == 1, middle.astype(F32), jnp.where(part == 2, low.astype(F32), 0.0)),
    ).astype(jnp.bfloat16)
    source = lax.broadcasted_iota(jnp.int32, (128, 256), 0)
    target = lax.broadcasted_iota(jnp.int32, (128, 256), 1)
    pick = jnp.where(target // 2 == source, 1.0, 0.0).astype(jnp.bfloat16)
    pieces = [
        jnp.dot(parts[:, 128 * m : 128 * (m + 1)], pick, preferred_element_type=F32) for m in range(width // 256)
    ]
    picked = jnp.concatenate(pieces, 1)
    return picked[0:1] + picked[1:2] + picked[2:3]


def neighbours(even_ref, even2_ref, odd2_ref):
    block = lax.axis_index("rows")
    is_even = lax.rem(block, 2) == 0
    is_low = lax.rem(block, 4) < 2
    even = even_ref[...]
    even2 = even2_ref[...]
    odd2 = odd2_ref[...]
    up = jnp.where(is_low, odd2, even2)
    down = jnp.where(is_low, even2, odd2)
    return jnp.where(is_even, up[2:4], even[2:4]), jnp.where(is_even, even[0:2], down[2:4]), up[1:2], down[0:1]


def between_body(
    flow_ref, face_ref, msg_ref, nest_ref, gain_ref, even_ref, odd2_ref, even2_ref, own_hx_ref, other_hx_ref,
    hx_below_ref, packet_ref, table_ref, h_ref, next_flow_ref, next_msg_ref, next_nest_ref, u_down_ref, hx_ref,
):
    g = table_ref.shape[0]
    n = g // 2
    half = lax.axis_index("sub")
    block = lax.axis_index("rows")
    is_first = block == 0
    is_last = block == lax.axis_size("rows") - 1
    nearfield = lax.axis_index("nest") == 1
    mine = pl.multiple_of(half * n, n)
    theirs = pl.multiple_of((1 - half) * n, n)
    hx_ref[pl.ds(mine, n)] = own_hx_ref[...]
    hx_ref[pl.ds(theirs, n)] = other_hx_ref[...]
    own = msg_ref[...]
    above, below, u_above2, t_below2 = neighbours(even_ref, even2_ref, odd2_ref)
    table = table_ref[...]
    face = face_ref[...]
    t_row = below[0:1]
    u_row = above[0:1]
    flow = flow_ref[...] + table[:, g - 1 : g] * t_row + table[:, 0:1] * u_row
    flux = face * flow
    gain = gain_ref[...]
    flux_above = above[1:2] + gain[2:3] * own[0:1] + gain[3:4] * u_above2
    h_below = hx_below_ref[0:1] + below[1:2] + gain[0:1] * t_below2 + gain[1:2] * own[2:3] - 0.5 * flux[g - 1 : g]
    hx_ref[...] = hx_ref[...] + 0.5 * (flux - prev_row(flux, flux_above))
    packet = packet_ref[0:1]
    for row, here in ((0, is_first), (g - 1, is_last)):
        value = hx_ref[row : row + 1]
        blended = 0.5 * value + 0.5 * packet
        hx_ref[row : row + 1] = jnp.where(jnp.logical_and(nearfield, here), blended, value)
    h = hx_ref[...]
    h_ref[...] = hx_ref[pl.ds(mine, n)]
    push = flow + 0.5 * face * (next_row(h, h_below) - h)
    next_flow, t_up, u_down = solve_lines(push, face, nest_ref[2:3], table)
    next_flow_ref[...] = next_flow
    rows, nest_rows = messages(next_flow, face, t_up, u_down, table, is_first)
    next_msg_ref[...] = rows
    u_down_ref[...] = u_down
    next_nest_ref[0:2] = nest_rows
    next_nest_ref[2:8] = jnp.zeros((6, face.shape[1]), F32)


def finish_body(
    flow_ref, even_ref, odd_ref, table_ref, face_ref, hx_ref, flow_x_ref,
    my_far, flow_x_far, h_far, edge_ref, before_ref, my_ref, h_ref, sems,
):
    copies = copies_of(flow_x_ref, flow_x_far, sems.at[0])
    for copy in copies:
        copy.start()
    g, width = flow_ref.shape
    n = g // 2
    half = lax.axis_index("sub")
    mine = pl.ds(pl.multiple_of(half * n, n), n)
    is_even = lax.rem(lax.axis_index("rows"), 2) == 0
    above = jnp.where(is_even, odd_ref[...], even_ref[...])
    below = jnp.where(is_even, even_ref[...], odd_ref[...])
    t_row = below[0:1]
    u_row = above[2:3]
    table = table_ref[mine]
    flow = flow_ref[mine] + table[:, g - 1 : g] * t_row + table[:, 0:1] * u_row
    my_ref[...] = flow
    for copy in copies_of(my_ref, my_far, sems.at[1]):
        copy.start()
        copies.append(copy)
    flux = face_ref[mine] * flow
    h_ref[...] = hx_ref[...] + 0.5 * (flux - prev_row(flux, 0.0))
    inner = pl.ds(8, n - 16)
    copies.append(pltpu.make_async_copy(h_ref.at[inner], h_far.at[inner], sems.at[2, 0]))
    copies[-1].start()
    edge_ref[0:8] = h_ref[0:8]
    edge_ref[8:16] = h_ref[n - 8 : n]
    flow_mid = flow_ref[n - 1 : n] + table_ref[n - 1 : n, g - 1 : g] * t_row + table_ref[n - 1 : n, 0:1] * u_row
    before_ref[0:1] = face_ref[n - 1 : n] * flow_mid
    before_ref[1:2] = above[3:4]
    before_ref[2:8] = jnp.zeros((6, width), F32)
    for copy in copies:
        copy.wait()


def finish_edge_body(h_in, edge_ref, before_ref, msg_ref, gain_ref, above2_ref, packet_ref, h_far, rows_ref, sems):
    n = h_far.shape[0]
    half = lax.axis_index("sub")
    block = lax.axis_index("rows")
    nearfield = lax.axis_index("nest") == 1
    is_first = jnp.logical_and(nearfield, jnp.logical_and(block == 0, half == 0))
    is_last = jnp.logical_and(nearfield, jnp.logical_and(block == lax.axis_size("rows") - 1, half == 1))
    flux_above = before_ref[1:2] + gain_ref[2:3] * msg_ref[0:1] + gain_ref[3:4] * above2_ref[...]
    before = jnp.where(half == 0, flux_above, before_ref[0:1])
    packet = packet_ref[...]
    edge = edge_ref[...]
    rows = row_iota(edge.shape)
    edge = jnp.where(rows == 0, edge - 0.5 * before, edge)
    blend = jnp.logical_or(jnp.logical_and(is_first, rows == 0), jnp.logical_and(is_last, rows == 15))
    rows_ref[...] = jnp.where(blend, 0.5 * edge + 0.5 * packet, edge)
    copies = [
        pltpu.make_async_copy(rows_ref.at[pl.ds(0, 8)], h_far.at[pl.ds(0, 8)], sems.at[0]),
        pltpu.make_async_copy(rows_ref.at[pl.ds(8, 8)], h_far.at[pl.ds(n - 8, 8)], sems.at[1]),
    ]
    for copy in copies:
        copy.start()
    for copy in copies:
        copy.wait()


def on_device(elevation, momentum_x, momentum_y, depth, wet_mask, inverse_x, inverse_y, nest_map):
    n, width = elevation.shape[1:]
    g = inverse_y.shape[-1]
    assert g == 2 * n and lax.axis_size("sub") == 2
    table_x = inverse_x[0]
    solve_flops = 2 * g * g * width * 2
    part = pltpu.VMEM((n, width), F32)
    slab = pltpu.VMEM((8, width), F32)
    dma = pltpu.SemaphoreType.DMA

    (wd,) = call(
        depth_body, [(n, width)], [depth[0], wet_mask[0]],
        [part, pltpu.VMEM((n, width), jnp.int32), dma((2, 4))], far=(0, 1),
    )
    other_wd = swap_halves(wd)
    buf, edge, height, flow_x = call(
        prepare_body, [(n + 8, width), (4, width), (n, width), (n, width)],
        [elevation[0], momentum_y[0], momentum_x[0], wd],
        [part, dma((3, 4))], far=(0, 1, 2), flops=int(0),
    )
    other = swap_halves(buf)
    cross = moved(edge, lambda k, s: (k + 1, 0) if s == 1 else (k - 1, 1))
    along = moved(edge, lambda k, s: (k + 1, 1) if s == 1 else (k - 1, 0))
    flow_x, hx, table_y, near_tables = call(
        across_first_body, [(n, width), (n, width), (g, g), (16, g)],
        [height, flow_x, wd, table_x, inverse_y[0], along], [part, part, dma((3,))], solve_flops, far=(4,),
    )
    (inner,) = call(faces_body, [(g, width)], [wd, other_wd], [pltpu.VMEM((g, width), F32)], flops=int(1e9))
    flow, face, msg, nest, gain = call(
        by_columns(lines_body, width, 256), [(g, width), (g, width), (4, width), (8, width), (8, width)],
        [buf, wd, other, other_wd, cross, along, table_y, near_tables, inner], [pltpu.VMEM((g, width), F32)], solve_flops,
    )
    other_hx = swap_halves(lax.optimization_barrier((hx, msg))[0])
    even = moved(msg, lambda k, s: (k ^ 1, s))
    (both,) = call(relay_body, [(4, width)], [msg, even], flops=int(3e9))
    even2 = moved(both, lambda k, s: (k ^ 2, s))
    odd2 = moved(both, lambda k, s: (((k + 2) ^ 2) - 2, s))
    (hx_below,) = call(
        across_below_body, [(8, width)], [cross, along, table_x], [slab] * 6
    )
    (packet,) = call(packet_body, [(1, width)], [nest, even, nest_map, hx, other_hx])
    packet = swap_nest(packet)
    height, flow, msg, nest, u_down = call(
        by_columns(between_body, width, 256), [(n, width), (g, width), (4, width), (8, width), (1, width)],
        [flow, face, msg, nest, gain, even, odd2, even2, hx, other_hx, hx_below, packet, table_y],
        [pltpu.VMEM((g, width), F32)], solve_flops,
    )
    even = moved(msg, lambda k, s: (k ^ 1, s))
    odd = moved(msg, lambda k, s: (((k + 1) ^ 1) - 1, s))
    above2 = moved(u_down, lambda k, s: (k + 2, s) if s == 0 else None)
    flow_x, hx = call(across, [(n, width), (n, width)], [height, flow_x, wd, table_x], [part, part], solve_flops)
    (packet,) = call(packet_body, [(1, width)], [nest, even, nest_map, hx, odd])
    packet = swap_nest(packet)
    flow_y, flow_x, height, edge, before = call(
        finish_body, [(n, width), (n, width), (n, width), (16, width), (8, width)],
        [flow, even, odd, table_y, face, hx, flow_x], [part, part, dma((3, 4))], far_outs=(0, 1, 2),
    )
    (height,) = call(
        finish_edge_body, [(n, width)], [height, edge, before, msg, gain, above2, packet],
        [pltpu.VMEM((16, width), F32), dma((2,))], far=(0,), far_outs=(0,), aliases={0: 0},
    )
    return height[None], flow_x[None], flow_y[None]


def solution(mesh):
    fields = P("nest", LINE, None)
    tables = P("nest", None, None, None)
    return jax.shard_map(
        on_device,
        mesh=mesh,
        in_specs=(fields,) * 5 + (tables, tables, P()),
        out_specs=(fields,) * 3,
        check_vma=False,
    )
```

```python
import jax
import jax.numpy as jnp
from jax import lax
from jax.experimental import pallas as pl
from jax.experimental.pallas import tpu as pltpu
from jax.sharding import PartitionSpec as P

LINE = ("rows", "sub")
VM = pl.BlockSpec(memory_space=pltpu.VMEM)
SM = pl.BlockSpec(memory_space=pltpu.SMEM)
FAR = pl.BlockSpec(memory_space=pltpu.HBM)
F32 = jnp.float32


def moved(value, target):
    blocks = lax.axis_size("rows")
    pairs = []
    for source in range(2 * blocks):
        there = target(source // 2, source % 2)
        if there is not None and 0 <= there[0] < blocks:
            pairs.append((source, 2 * there[0] + there[1]))
    return lax.ppermute(value, LINE, pairs)


def swap_halves(value):
    return lax.ppermute(value, "sub", [(0, 1), (1, 0)])


def swap_nest(value):
    return lax.ppermute(value, "nest", [(0, 1), (1, 0)])


def call(body, outs, ins, scratch=(), flops=0, far=(), far_outs=(), vmem=8, aliases=None):
    shapes = [o if isinstance(o, jax.ShapeDtypeStruct) else jax.ShapeDtypeStruct(o, F32) for o in outs]
    nbytes = sum(4 * x.size for i, x in enumerate(ins) if i not in far) + sum(4 * x.size for x in shapes)

    def spec(i, x, others):
        if i in others:
            return FAR
        return SM if x.dtype == jnp.int32 and x.size < 16 else VM

    return pl.pallas_call(
        body,
        out_shape=shapes,
        in_specs=[spec(i, x, far) for i, x in enumerate(ins)],
        out_specs=[spec(i, x, far_outs) for i, x in enumerate(shapes)],
        scratch_shapes=list(scratch),
        input_output_aliases=aliases or {},
        cost_estimate=pl.CostEstimate(flops=flops, bytes_accessed=nbytes, transcendentals=0),
        compiler_params=pltpu.CompilerParams(vmem_limit_bytes=vmem * 2**20),
    )(*[pltpu.with_memory_space_constraint(x, pltpu.HBM) if i in far else x for i, x in enumerate(ins)])


def by_columns(body, width, step):
    def run(*refs):
        for start in range(0, width, step):
            body(*[ref.at[:, pl.ds(start, step)] if ref.shape[-1] == width else ref for ref in refs])

    return run


def face_of(a, b):
    return jnp.where(jnp.logical_and(a > 0.0, b > 0.0), 0.5 * (a + b), 0.0)


def split(a):
    high = a.astype(jnp.bfloat16)
    low = (a - high.astype(F32)).astype(jnp.bfloat16)
    return high, low


def stacked(a):
    high, low = split(a)
    return jnp.concatenate([jnp.concatenate([high, high], 1), jnp.concatenate([low, jnp.zeros_like(low)], 1)], 0)


def folded(product):
    rows = product.shape[0] // 2
    return product[:rows] + product[rows:]


def matmul(a, b):
    return folded(jnp.dot(stacked(a), jnp.concatenate(split(b), 0), preferred_element_type=F32))


def matmul_t(a, b):
    wide = jnp.concatenate(split(b), 1)
    return folded(
        lax.dot_general(stacked(a), wide, (((1,), (1,)), ((), ())), preferred_element_type=F32)
    )


def row_iota(shape):
    return lax.broadcasted_iota(jnp.int32, shape, 0)


def next_row(x, edge):
    n = x.shape[0]
    return jnp.where(row_iota(x.shape) == n - 1, edge, pltpu.roll(x, n - 1, 0))


def prev_row(x, edge):
    return jnp.where(row_iota(x.shape) == 0, edge, pltpu.roll(x, 1, 0))


def copies_of(source, target, sems, parts=4):
    step = source.shape[0] // parts
    return [
        pltpu.make_async_copy(source.at[pl.ds(p * step, step)], target.at[pl.ds(p * step, step)], sems.at[p])
        for p in range(parts)
    ]


def depth_body(depth_far, wet_far, wd_ref, depth_ref, wet_ref, sems):
    copies = copies_of(depth_far, depth_ref, sems.at[0]) + copies_of(wet_far, wet_ref, sems.at[1])
    for copy in copies:
        copy.start()
    for copy in copies:
        copy.wait()
    wd_ref[...] = depth_ref[...] * wet_ref[...].astype(F32)


def prepare_body(h_far, my_far, mx_far, wd_ref, buf_ref, edge_ref, h_ref, mx_ref, my_ref, sems):
    n, width = h_ref.shape
    fetched = []
    for i, (far, near) in enumerate([(h_far, h_ref), (my_far, my_ref), (mx_far, mx_ref)]):
        fetched += copies_of(far, near, sems.at[i])
    for copy in fetched:
        copy.start()
    for copy in fetched:
        copy.wait()
    wd = wd_ref[...]
    h = h_ref[...]
    buf_ref[0:n] = my_ref[...] + 0.5 * face_of(wd, next_row(wd, 0.0)) * (next_row(h, 0.0) - h)
    buf_ref[n : n + 8] = jnp.concatenate([h[0:1], h[n - 1 : n], jnp.zeros((6, width), F32)], 0)
    outward = jnp.where(lax.axis_index("sub") == 0, wd[0:1], wd[n - 1 : n])
    edge_ref[...] = jnp.concatenate([h[0:1], outward, mx_ref[0:1], face_of(wd[0:1], wd[1:2])], 0)


def across(h_ref, mx_ref, wd_ref, table_ref, flow_ref, hx_ref, push_ref, first_ref):
    n, width = h_ref.shape
    group = table_ref.shape[-1]
    h = h_ref[...]
    wd = wd_ref[...]
    lane = lax.broadcasted_iota(jnp.int32, wd.shape, 1)
    face = face_of(wd, jnp.where(lane == width - 1, 0.0, pltpu.roll(wd, width - 1, 1)))
    coef = 0.5 * face * face
    push = mx_ref[...] + 0.5 * face * (pltpu.roll(h, width - 1, 1) - h)
    push_ref[...] = push
    for b in range(width // group):
        cols = slice(b * group, (b + 1) * group)
        first_ref[:, cols] = matmul_t(push_ref[:, cols], table_ref[b])
    first = first_ref[...]
    operated = (
        first
        + coef * (first - pltpu.roll(first, width - 1, 1))
        + pltpu.roll(coef, 1, 1) * (first - pltpu.roll(first, 1, 1))
    )
    push_ref[...] = push - operated
    for b in range(width // group):
        cols = slice(b * group, (b + 1) * group)
        flow_ref[:, cols] = first_ref[:, cols] + matmul_t(push_ref[:, cols], table_ref[b])
    flux = face * flow_ref[...]
    hx_ref[...] = h + 0.5 * (flux - pltpu.roll(flux, 1, 1))


def across_first_body(
    h_ref, mx_ref, wd_ref, table_ref, tables_far, along_ref,
    flow_ref, hx_ref, line_table_ref, near_tables_ref, push_ref, first_ref, sems,
):
    block = lax.axis_index("rows")
    group = line_table_ref.shape[0]
    up = jnp.maximum(block - 1, 0)
    down = jnp.minimum(block + 1, tables_far.shape[0] - 1)
    fetches = [
        pltpu.make_async_copy(tables_far.at[block], line_table_ref, sems.at[0]),
        pltpu.make_async_copy(tables_far.at[up, pl.ds(group - 8, 8)], near_tables_ref.at[pl.ds(0, 8)], sems.at[1]),
        pltpu.make_async_copy(tables_far.at[down, pl.ds(0, 8)], near_tables_ref.at[pl.ds(8, 8)], sems.at[2]),
    ]
    for fetch in fetches:
        fetch.start()
    across(h_ref, mx_ref, wd_ref, table_ref, flow_ref, hx_ref, push_ref, first_ref)
    for fetch in fetches:
        fetch.wait()


def across_below_body(cross_ref, along_ref, table_ref, hx_ref, h_ref, mx_ref, wd_ref, flow_ref, push_ref, first_ref):
    below = jnp.where(lax.axis_index("sub") == 0, along_ref[...], cross_ref[...])
    h_ref[...] = jnp.broadcast_to(below[0:1], h_ref.shape)
    wd_ref[...] = jnp.broadcast_to(below[1:2], h_ref.shape)
    mx_ref[...] = jnp.broadcast_to(below[2:3], h_ref.shape)
    across(h_ref, mx_ref, wd_ref, table_ref, flow_ref, hx_ref, push_ref, first_ref)


def relay_body(msg_ref, even_ref, out_ref):
    is_even = lax.rem(lax.axis_index("rows"), 2) == 0
    even = even_ref[...]
    msg = msg_ref[...]
    passed = jnp.where(is_even, even[2:4], even[0:2])
    out_ref[...] = jnp.concatenate([msg[0:1], msg[2:3], passed], 0)


def packet_body(nest_ref, even_ref, map_ref, hx_ref, other_ref, packet_ref):
    n = hx_ref.shape[0]
    lower = lax.axis_index("sub") == 0
    is_first = lax.axis_index("rows") == 0
    top = hx_ref[0:1]
    bottom = hx_ref[n - 1 : n]
    if other_ref.shape == hx_ref.shape:
        top, bottom = jnp.where(lower, top, other_ref[0:1]), jnp.where(lower, other_ref[n - 1 : n], bottom)
    row = jnp.where(is_first, top, bottom) + nest_ref[0:1] + nest_ref[1:2] * nest_factor(even_ref)
    base = jnp.min(map_ref[0, 1:2, 0:128].astype(F32)).astype(jnp.int32)
    packet_ref[...] = upsampled(row, base)


def nest_factor(even_ref):
    return jnp.where(lax.axis_index("rows") == 0, even_ref[0:1], even_ref[2:3])


def solve_lines(push, face, face_above, table):
    coef = 0.5 * face * face
    coef_above = 0.5 * face_above * face_above
    first = matmul(table, push)
    step = coef * (first - next_row(first, 0.0))
    flow = first + matmul(table, push - first - step + prev_row(step, -(coef_above * first[0:1])))
    g = push.shape[0]
    t_up = coef_above * first[0:1]
    u_down = coef[g - 1 : g] * first[g - 1 : g]
    return flow, t_up, u_down


def messages(flow, face, t_up, u_down, table, is_first):
    g = flow.shape[0]
    half_top = 0.5 * face[0:1]
    side = 0.5 * face[g - 2 : g - 1]
    rows = [t_up, half_top * flow[0:1], u_down, face[g - 1 : g] * flow[g - 1 : g]]
    nest_base = jnp.where(is_first, rows[1], -(side * flow[g - 2 : g - 1]))
    nest_coef = jnp.where(is_first, half_top * table[0:1, g - 1 : g], -(side * table[g - 2 : g - 1, 0:1]))
    return jnp.concatenate(rows, 0), jnp.concatenate([nest_base, nest_coef], 0)


def faces_body(own_wd_ref, other_wd_ref, face_ref, wd_ref):
    n = own_wd_ref.shape[0]
    half = lax.axis_index("sub")
    wd_ref[pl.ds(pl.multiple_of(half * n, n), n)] = own_wd_ref[...]
    wd_ref[pl.ds(pl.multiple_of((1 - half) * n, n), n)] = other_wd_ref[...]
    wd = wd_ref[...]
    face_ref[...] = face_of(wd, next_row(wd, 0.0))


def lines_body(
    own_ref, own_wd_ref, other_ref, other_wd_ref, cross_ref, along_ref, table_ref, near_tables_ref, inner_ref,
    flow_ref, face_ref, msg_ref, nest_ref, gain_ref, push_ref,
):
    g = table_ref.shape[0]
    n = g // 2
    half = lax.axis_index("sub")
    lower = half == 0
    is_first = lax.axis_index("rows") == 0
    mine = pl.multiple_of(half * n, n)
    theirs = pl.multiple_of((1 - half) * n, n)
    push_ref[pl.ds(mine, n)] = own_ref[0:n]
    push_ref[pl.ds(theirs, n)] = other_ref[0:n]
    own = own_ref[n : n + 8]
    other = other_ref[n : n + 8]
    cross = cross_ref[...]
    along = along_ref[...]
    top = jnp.where(lower, own, other)
    bottom = jnp.where(lower, other, own)
    below = jnp.where(lower, along, cross)
    above = jnp.where(lower, cross, along)
    wd_last = jnp.where(lower, other_wd_ref[n - 1 : n], own_wd_ref[n - 1 : n])
    face_ref[...] = inner_ref[...]
    face_ref[g - 1 : g] = face_of(wd_last, below[1:2])
    face_above = face_of(above[1:2], jnp.where(lower, own_wd_ref[0:1], other_wd_ref[0:1]))
    push_ref[n - 1 : n] += 0.5 * face_ref[n - 1 : n] * (bottom[0:1] - top[1:2])
    push_ref[g - 1 : g] += 0.5 * face_ref[g - 1 : g] * (below[0:1] - bottom[1:2])
    face = face_ref[...]
    table = table_ref[...]
    flow, t_up, u_down = solve_lines(push_ref[...], face, face_above, table)
    flow_ref[...] = flow
    rows, nest_rows = messages(flow, face, t_up, u_down, table, is_first)
    msg_ref[...] = rows
    nest_ref[0:1] = nest_rows[0:1]
    nest_ref[1:2] = nest_rows[1:2]
    half_below = 0.5 * below[3:4]
    near = near_tables_ref[...]
    gain_ref[0:1] = half_below * near[8:9, g - 1 : g]
    gain_ref[1:2] = half_below * near[8:9, 0:1]
    gain_ref[2:3] = face_above * near[7:8, g - 1 : g]
    gain_ref[3:4] = face_above * near[7:8, 0:1]
    gain_ref[4:8] = jnp.zeros((4, half_below.shape[1]), F32)
    nest_ref[2:3] = face_above
    nest_ref[3:8] = jnp.zeros((5, face.shape[1]), F32)


def upsampled(row, base):
    width = row.shape[1]
    rolled = pltpu.roll(jnp.broadcast_to(row, (8, width)), lax.rem(width - base, width), 1)
    high = rolled.astype(jnp.bfloat16)
    middle, low = split(rolled - high.astype(F32))
    part = lax.broadcasted_iota(jnp.int32, rolled.shape, 0)
    parts = jnp.where(
        part == 0,
        high.astype(F32),
        jnp.where(part == 1, middle.astype(F32), jnp.where(part == 2, low.astype(F32), 0.0)),
    ).astype(jnp.bfloat16)
    source = lax.broadcasted_iota(jnp.int32, (128, 256), 0)
    target = lax.broadcasted_iota(jnp.int32, (128, 256), 1)
    pick = jnp.where(target // 2 == source, 1.0, 0.0).astype(jnp.bfloat16)
    pieces = [
        jnp.dot(parts[:, 128 * m : 128 * (m + 1)], pick, preferred_element_type=F32) for m in range(width // 256)
    ]
    picked = jnp.concatenate(pieces, 1)
    return picked[0:1] + picked[1:2] + picked[2:3]


def neighbours(even_ref, even2_ref, odd2_ref):
    block = lax.axis_index("rows")
    is_even = lax.rem(block, 2) == 0
    is_low = lax.rem(block, 4) < 2
    even = even_ref[...]
    even2 = even2_ref[...]
    odd2 = odd2_ref[...]
    up = jnp.where(is_low, odd2, even2)
    down = jnp.where(is_low, even2, odd2)
    return jnp.where(is_even, up[2:4], even[2:4]), jnp.where(is_even, even[0:2], down[2:4]), up[1:2], down[0:1]


def between_body(
    flow_ref, face_ref, msg_ref, nest_ref, gain_ref, even_ref, odd2_ref, even2_ref, own_hx_ref, other_hx_ref,
    hx_below_ref, packet_ref, table_ref, h_ref, next_flow_ref, next_msg_ref, next_nest_ref, u_down_ref, hx_ref,
):
    g = table_ref.shape[0]
    n = g // 2
    half = lax.axis_index("sub")
    block = lax.axis_index("rows")
    is_first = block == 0
    is_last = block == lax.axis_size("rows") - 1
    nearfield = lax.axis_index("nest") == 1
    mine = pl.multiple_of(half * n, n)
    theirs = pl.multiple_of((1 - half) * n, n)
    hx_ref[pl.ds(mine, n)] = own_hx_ref[...]
    hx_ref[pl.ds(theirs, n)] = other_hx_ref[...]
    own = msg_ref[...]
    above, below, u_above2, t_below2 = neighbours(even_ref, even2_ref, odd2_ref)
    table = table_ref[...]
    face = face_ref[...]
    t_row = below[0:1]
    u_row = above[0:1]
    flow = flow_ref[...] + table[:, g - 1 : g] * t_row + table[:, 0:1] * u_row
    flux = face * flow
    gain = gain_ref[...]
    flux_above = above[1:2] + gain[2:3] * own[0:1] + gain[3:4] * u_above2
    h_below = hx_below_ref[0:1] + below[1:2] + gain[0:1] * t_below2 + gain[1:2] * own[2:3] - 0.5 * flux[g - 1 : g]
    hx_ref[...] = hx_ref[...] + 0.5 * (flux - prev_row(flux, flux_above))
    packet = packet_ref[0:1]
    for row, here in ((0, is_first), (g - 1, is_last)):
        value = hx_ref[row : row + 1]
        blended = 0.5 * value + 0.5 * packet
        hx_ref[row : row + 1] = jnp.where(jnp.logical_and(nearfield, here), blended, value)
    h = hx_ref[...]
    h_ref[...] = hx_ref[pl.ds(mine, n)]
    push = flow + 0.5 * face * (next_row(h, h_below) - h)
    next_flow, t_up, u_down = solve_lines(push, face, nest_ref[2:3], table)
    next_flow_ref[...] = next_flow
    rows, nest_rows = messages(next_flow, face, t_up, u_down, table, is_first)
    next_msg_ref[...] = rows
    u_down_ref[...] = u_down
    next_nest_ref[0:2] = nest_rows
    next_nest_ref[2:8] = jnp.zeros((6, face.shape[1]), F32)


def finish_body(
    flow_ref, even_ref, odd_ref, table_ref, face_ref, hx_ref, flow_x_ref,
    my_far, flow_x_far, h_far, edge_ref, before_ref, my_ref, h_ref, sems,
):
    copies = copies_of(flow_x_ref, flow_x_far, sems.at[0])
    for copy in copies:
        copy.start()
    g, width = flow_ref.shape
    n = g // 2
    half = lax.axis_index("sub")
    mine = pl.ds(pl.multiple_of(half * n, n), n)
    is_even = lax.rem(lax.axis_index("rows"), 2) == 0
    above = jnp.where(is_even, odd_ref[...], even_ref[...])
    below = jnp.where(is_even, even_ref[...], odd_ref[...])
    t_row = below[0:1]
    u_row = above[2:3]
    table = table_ref[mine]
    flow = flow_ref[mine] + table[:, g - 1 : g] * t_row + table[:, 0:1] * u_row
    my_ref[...] = flow
    for copy in copies_of(my_ref, my_far, sems.at[1]):
        copy.start()
        copies.append(copy)
    flux = face_ref[mine] * flow
    h_ref[...] = hx_ref[...] + 0.5 * (flux - prev_row(flux, 0.0))
    inner = pl.ds(8, n - 16)
    copies.append(pltpu.make_async_copy(h_ref.at[inner], h_far.at[inner], sems.at[2, 0]))
    copies[-1].start()
    edge_ref[0:8] = h_ref[0:8]
    edge_ref[8:16] = h_ref[n - 8 : n]
    flow_mid = flow_ref[n - 1 : n] + table_ref[n - 1 : n, g - 1 : g] * t_row + table_ref[n - 1 : n, 0:1] * u_row
    before_ref[0:1] = face_ref[n - 1 : n] * flow_mid
    before_ref[1:2] = above[3:4]
    before_ref[2:8] = jnp.zeros((6, width), F32)
    for copy in copies:
        copy.wait()


def finish_edge_body(h_in, edge_ref, before_ref, msg_ref, gain_ref, above2_ref, packet_ref, h_far, rows_ref, sems):
    n = h_far.shape[0]
    half = lax.axis_index("sub")
    block = lax.axis_index("rows")
    nearfield = lax.axis_index("nest") == 1
    is_first = jnp.logical_and(nearfield, jnp.logical_and(block == 0, half == 0))
    is_last = jnp.logical_and(nearfield, jnp.logical_and(block == lax.axis_size("rows") - 1, half == 1))
    flux_above = before_ref[1:2] + gain_ref[2:3] * msg_ref[0:1] + gain_ref[3:4] * above2_ref[...]
    before = jnp.where(half == 0, flux_above, before_ref[0:1])
    packet = packet_ref[...]
    edge = edge_ref[...]
    rows = row_iota(edge.shape)
    edge = jnp.where(rows == 0, edge - 0.5 * before, edge)
    blend = jnp.logical_or(jnp.logical_and(is_first, rows == 0), jnp.logical_and(is_last, rows == 15))
    rows_ref[...] = jnp.where(blend, 0.5 * edge + 0.5 * packet, edge)
    copies = [
        pltpu.make_async_copy(rows_ref.at[pl.ds(0, 8)], h_far.at[pl.ds(0, 8)], sems.at[0]),
        pltpu.make_async_copy(rows_ref.at[pl.ds(8, 8)], h_far.at[pl.ds(n - 8, 8)], sems.at[1]),
    ]
    for copy in copies:
        copy.start()
    for copy in copies:
        copy.wait()


def on_device(elevation, momentum_x, momentum_y, depth, wet_mask, inverse_x, inverse_y, nest_map):
    n, width = elevation.shape[1:]
    g = inverse_y.shape[-1]
    assert g == 2 * n and lax.axis_size("sub") == 2
    table_x = inverse_x[0]
    solve_flops = 2 * g * g * width * 2
    part = pltpu.VMEM((n, width), F32)
    slab = pltpu.VMEM((8, width), F32)
    dma = pltpu.SemaphoreType.DMA

    (wd,) = call(
        depth_body, [(n, width)], [depth[0], wet_mask[0]],
        [part, pltpu.VMEM((n, width), jnp.int32), dma((2, 4))], far=(0, 1),
    )
    other_wd = swap_halves(wd)
    buf, edge, height, flow_x = call(
        prepare_body, [(n + 8, width), (4, width), (n, width), (n, width)],
        [elevation[0], momentum_y[0], momentum_x[0], wd],
        [part, dma((3, 4))], far=(0, 1, 2), flops=int(0),
    )
    other = swap_halves(buf)
    cross = moved(edge, lambda k, s: (k + 1, 0) if s == 1 else (k - 1, 1))
    along = moved(edge, lambda k, s: (k + 1, 1) if s == 1 else (k - 1, 0))
    flow_x, hx, table_y, near_tables = call(
        across_first_body, [(n, width), (n, width), (g, g), (16, g)],
        [height, flow_x, wd, table_x, inverse_y[0], along], [part, part, dma((3,))], solve_flops, far=(4,),
    )
    (inner,) = call(faces_body, [(g, width)], [wd, other_wd], [pltpu.VMEM((g, width), F32)], flops=int(1e9))
    flow, face, msg, nest, gain = call(
        by_columns(lines_body, width, 256), [(g, width), (g, width), (4, width), (8, width), (8, width)],
        [buf, wd, other, other_wd, cross, along, table_y, near_tables, inner], [pltpu.VMEM((g, width), F32)], solve_flops,
    )
    other_hx = swap_halves(lax.optimization_barrier((hx, msg))[0])
    even = moved(msg, lambda k, s: (k ^ 1, s))
    (both,) = call(relay_body, [(4, width)], [msg, even], flops=int(3e9))
    even2 = moved(both, lambda k, s: (k ^ 2, s))
    odd2 = moved(both, lambda k, s: (((k + 2) ^ 2) - 2, s))
    (hx_below,) = call(
        across_below_body, [(8, width)], [cross, along, table_x], [slab] * 6
    )
    (packet,) = call(packet_body, [(1, width)], [nest, even, nest_map, hx, other_hx])
    packet = swap_nest(packet)
    height, flow, msg, nest, u_down = call(
        by_columns(between_body, width, 256), [(n, width), (g, width), (4, width), (8, width), (1, width)],
        [flow, face, msg, nest, gain, even, odd2, even2, hx, other_hx, hx_below, packet, table_y],
        [pltpu.VMEM((g, width), F32)], solve_flops,
    )
    even = moved(msg, lambda k, s: (k ^ 1, s))
    odd = moved(msg, lambda k, s: (((k + 1) ^ 1) - 1, s))
    above2 = moved(u_down, lambda k, s: (k + 2, s) if s == 0 else None)
    flow_x, hx = call(across, [(n, width), (n, width)], [height, flow_x, wd, table_x], [part, part], solve_flops)
    (packet,) = call(packet_body, [(1, width)], [nest, even, nest_map, hx, even])
    packet = swap_nest(packet)
    flow_y, flow_x, height, edge, before = call(
        finish_body, [(n, width), (n, width), (n, width), (16, width), (8, width)],
        [flow, even, odd, table_y, face, hx, flow_x], [part, part, dma((3, 4))], far_outs=(0, 1, 2),
    )
    (height,) = call(
        finish_edge_body, [(n, width)], [height, edge, before, msg, gain, above2, packet],
        [pltpu.VMEM((16, width), F32), dma((2,))], far=(0,), far_outs=(0,), aliases={0: 0},
    )
    return height[None], flow_x[None], flow_y[None]


def solution(mesh):
    fields = P("nest", LINE, None)
    tables = P("nest", None, None, None)
    return jax.shard_map(
        on_device,
        mesh=mesh,
        in_specs=(fields,) * 5 + (tables, tables, P()),
        out_specs=(fields,) * 3,
        check_vma=False,
    )
```
